256 devices in a mesh: dp: 32 (over z_lo, x, core), group: 8 (over y, z_hi).
Axes of the slice: x: 4, y: 4, z: 8 (z_hi: 2, z_lo: 4; z = z_hi * 4 + z_lo), core: 2. Of those that a mesh axis runs over, the one named last changes fastest.
Arguments:
- tokens: bfloat16 [32768, 7168], P('dp', 'group'), may hold values from -6 to 6
- proj_in: bfloat16 [32, 1024, 2, 7168], P(None, 'dp', None, 'group'), may hold values from -0.0625 to 0.0625
- proj_out: bfloat16 [32, 1024, 7168], P(None, 'dp', 'group'), may hold values from -0.1875 to 0.1875
- expert_list: int32 [32, 2], replicated, may hold values from 0 to 31, as said below
- block_pattern: int32 [32, 2, 8], replicated, may hold values from 0 to 1, as said below
- route_weight: float32 [32768, 2], P('dp'), may hold values from 0.1 to 1
Outputs:
- mixed: bfloat16 [32768, 7168], P('dp', 'group')
The draws below stay inside these ranges and needn't reach their ends.
Inputs may be any that keep to these rules, and one draw needn't show every extreme that they name: `expert_list`: each row names 2 different experts of the window. `block_pattern`: 1 where the list slot's expert acts on that block of 128 tokens, else 0; the share of ones differs from token group to token group, and in every draw some token group has every block of every slot set.
All inputs are finite; a program needn't handle non-finite values.
Results may differ from the reference program's by a relative error of at most 0.025.
Values may be sent and summed in bfloat16 or wider, within the bound.
A program may use at most 128 MiB of HBM per device.

```python
import math
import jax
import jax.numpy as jnp
from jax import lax

D = 7168
FF = 1024
EXPERTS = 32
LIST = 2
BLOCK = 128
TOK_DEV = 1024
NBLK = 8
TOKENS = 32768
N_DP = 32
N_GROUP = 8


def draw_expert_list(key, part):
    row_keys = jax.random.split(jax.random.fold_in(key, 11), N_DP)
    chosen = jax.vmap(lambda one_key: jax.random.permutation(one_key, EXPERTS)[:LIST])(row_keys)
    return chosen.astype(jnp.int32)


def draw_block_pattern(key, part):
    key_level = jax.random.fold_in(key, 21)
    key_bits = jax.random.fold_in(key, 22)
    key_busy = jax.random.fold_in(key, 23)
    fill_level = jax.random.randint(key_level, (N_DP, 1, 1), 1, 9)
    busiest = jax.random.randint(key_busy, (), 0, N_DP)
    row_index = jnp.arange(N_DP, dtype=jnp.int32)[:, None, None]
    fill_level = jnp.where(row_index == busiest, 8, fill_level)
    random_bits = jax.random.randint(key_bits, (N_DP, LIST, NBLK), 0, 8)
    return (random_bits < fill_level).astype(jnp.int32)


def levels(rng, extent, pieces, low, largest):
    factor_of, own = 1.0, jax.random.fold_in(rng, 6)
    for dim, shards_of in pieces:
        heights = jnp.exp(jax.random.uniform(jax.random.fold_in(own, dim), (shards_of,), jnp.float32, low / len(pieces), largest / len(pieces)))
        factor_of = factor_of * jnp.repeat(heights, extent[dim] // shards_of).reshape([-1 if axis == dim else 1 for axis in range(len(extent))])
    return factor_of


def centred(rng, shape, spread, reach, shards=(), kind=jnp.bfloat16):
    result = jax.random.normal(rng, shape, jnp.float32) * spread
    if len(shards) > 0:
        result = levels(rng, shape, shards, -0.22, 0.18) * result
    return jnp.clip(result, min=-reach, max=reach).astype(kind)


def setup_inputs(seed: int = 0) -> dict:
    splits = jax.random.split(jax.random.key(seed), 7)
    return {
        "tokens": centred(splits[0], (TOKENS, D), 1.0, 6.0, ((0, 32), (1, 8))),
        "proj_in": centred(splits[1], (EXPERTS, FF, 2, D), D ** -0.5, 0.0625, ((1, 32), (3, 8))),
        "proj_out": centred(splits[2], (EXPERTS, FF, D), FF ** -0.5, 0.1875, ((1, 32), (2, 8))),
        "expert_list": draw_expert_list(jax.random.fold_in(splits[6], 71), 0),
        "block_pattern": draw_block_pattern(jax.random.fold_in(splits[6], 71), 0),
        "route_weight": jnp.clip(jnp.exp(math.log(1.0) - 2.3025851 * jax.random.uniform(splits[5], (TOKENS, LIST), jnp.float32) ** levels(splits[5], (TOKENS, LIST), ((0, 32),), -0.2, 0.2)), 0.1, 1.0),
    }


def reference(tokens, proj_in, proj_out, expert_list, block_pattern, route_weight):
    group_width = D // N_GROUP
    group_rows = tokens.reshape(N_DP, TOK_DEV, D)
    group_weights = route_weight.reshape(N_DP, TOK_DEV, LIST)

    def one_group(inputs):
        token_rows, listed, pattern, weights_here = inputs
        block_mask = jnp.repeat(pattern, BLOCK, axis=1).astype(jnp.float32)
        combined = jnp.zeros((TOK_DEV, D), jnp.float32)
        for list_slot in range(LIST):
            expert = listed[list_slot].astype(jnp.int32)
            weight_in = lax.dynamic_index_in_dim(proj_in, expert, 0, keepdims=False)
            weight_out = lax.dynamic_index_in_dim(proj_out, expert, 0, keepdims=False)
            gate_up = jnp.zeros((TOK_DEV, FF * 2), jnp.float32)
            for column_part in range(N_GROUP):
                low = column_part * group_width
                token_cols = token_rows[:, low:low + group_width]
                weight_cols = weight_in[:, :, low:low + group_width].reshape(FF * 2, group_width)
                partial_value = jnp.dot(token_cols, weight_cols.T, preferred_element_type=jnp.float32)
                rounded = lax.optimization_barrier(partial_value.astype(jnp.bfloat16))
                gate_up = gate_up + rounded.astype(jnp.float32)
            gate_up = gate_up.reshape(TOK_DEV, FF, 2)
            token_scale = weights_here[:, list_slot] * block_mask[list_slot]
            hidden = (token_scale[:, None] * jax.nn.silu(gate_up[:, :, 0]) * gate_up[:, :, 1]).astype(jnp.bfloat16)
            combined = combined + jnp.dot(hidden, weight_out, preferred_element_type=jnp.float32)
        return combined.astype(jnp.bfloat16)

    mixed = lax.map(one_group, (group_rows, expert_list, block_pattern, group_weights))
    return mixed.reshape(TOKENS, D)
```

```python
import jax
import jax.numpy as jnp
from jax import lax
from jax.sharding import PartitionSpec as P


def on_device(tokens, proj_in, proj_out, expert_list, block_pattern, route_weight):
    group_size = lax.axis_size("group")
    n_dp = lax.axis_size("dp")
    dp_index = lax.axis_index("dp")
    row_count, width_here = tokens.shape
    slots = expert_list.shape[1]
    ff_here = proj_in.shape[1]
    block_rows = row_count // block_pattern.shape[2]

    own_pattern = lax.dynamic_index_in_dim(block_pattern, dp_index, 0, keepdims=False)
    block_mask = jnp.repeat(own_pattern, block_rows, axis=1).astype(jnp.float32)
    token_scale = route_weight.T * block_mask

    send_in = jnp.take(proj_in, expert_list, axis=0).transpose(0, 1, 3, 2, 4)
    send_out = jnp.take(proj_out, expert_list, axis=0)

    gathered = []
    weights_out = []
    pending = tokens
    for slot in range(slots):
        pending, piece = lax.optimization_barrier((pending, send_in[:, slot]))
        weight_in = lax.all_to_all(piece, "dp", 0, 0, tiled=True).reshape(-1, width_here)
        partial_here = jnp.dot(weight_in, tokens.T, preferred_element_type=jnp.float32)
        partial_here = partial_here.astype(jnp.bfloat16)
        shares = lax.psum_scatter(partial_here, "group", scatter_dimension=0, tiled=True)
        gathered.append(shares)
        pending = partial_here
    for slot in range(slots):
        pending, piece = lax.optimization_barrier((pending, send_out[:, slot]))
        weight_out = lax.all_to_all(piece, "dp", 0, 0, tiled=True)
        weights_out.append(weight_out.reshape(-1, width_here))
        pending = weight_out

    combined = None
    for slot in range(slots):
        shares = gathered[slot].astype(jnp.float32).reshape(n_dp // group_size, 2, ff_here, row_count)
        hidden = (token_scale[slot] * jax.nn.silu(shares[:, 0]) * shares[:, 1]).astype(jnp.bfloat16)
        hidden = lax.all_gather(hidden.reshape(-1, row_count), "group", axis=0, tiled=True)
        term = lax.dot_general(
            hidden, weights_out[slot], (((0,), (0,)), ((), ())), preferred_element_type=jnp.float32
        )
        combined = term if combined is None else combined + term
    return combined.astype(jnp.bfloat16)


def solution(mesh):
    return jax.shard_map(
        on_device,
        mesh=mesh,
        in_specs=(
            P("dp", "group"),
            P(None, "dp", None, "group"),
            P(None, "dp", "group"),
            P(),
            P(),
            P("dp", None),
        ),
        out_specs=P("dp", "group"),
        check_vma=False,
    )
```

```python
import jax
import jax.numpy as jnp
from jax import lax
from jax.sharding import PartitionSpec as P


Y_PARTS = 4


def _perm(size, fn):
    return [(j, fn(j)) for j in range(size)]


def _y_shift(size, dy):
    z_parts = size // Y_PARTS
    return _perm(size, lambda j: ((j // z_parts + dy) % Y_PARTS) * z_parts + j % z_parts)


def _z_flip(size):
    return _perm(size, lambda j: j ^ 1)


def group_reduce_scatter(x):
    size = lax.axis_size("group")
    j = lax.axis_index("group")
    y, zh = j // 2, j % 2
    rows = x.shape[0] // Y_PARTS
    half = rows // 2

    def block(yy):
        return lax.dynamic_slice_in_dim(x, (yy % Y_PARTS) * rows, rows, 0)

    far = block(y + 2)
    up = lax.ppermute(block(y + 1), "group", _y_shift(size, 1))
    down = lax.ppermute(block(y - 1), "group", _y_shift(size, -1))
    up_far = lax.ppermute(far[:half], "group", _y_shift(size, 1))
    down_far = lax.ppermute(far[half:], "group", _y_shift(size, -1))
    relay_up = lax.ppermute(up_far, "group", _y_shift(size, 1))
    relay_down = lax.ppermute(down_far, "group", _y_shift(size, -1))
    f32 = jnp.float32
    y_sum = (
        block(y).astype(f32) + up.astype(f32) + down.astype(f32)
        + jnp.concatenate([relay_up, relay_down], axis=0).astype(f32)
    )
    mine = lax.dynamic_slice_in_dim(y_sum, zh * half, half, 0)
    other = lax.dynamic_slice_in_dim(y_sum, (1 - zh) * half, half, 0)
    return mine + lax.ppermute(other.astype(jnp.bfloat16), "group", _z_flip(size)).astype(f32)


def group_all_gather(h):
    size = lax.axis_size("group")
    j = lax.axis_index("group")
    y, zh = j // 2, j % 2
    n = h.shape[0]
    partner = lax.ppermute(h, "group", _z_flip(size))
    pair = jnp.where(zh == 0, jnp.concatenate([h, partner]), jnp.concatenate([partner, h]))
    from_down = lax.ppermute(pair, "group", _y_shift(size, 1))
    from_up = lax.ppermute(pair, "group", _y_shift(size, -1))
    far_a = lax.ppermute(from_down[:n], "group", _y_shift(size, 1))
    far_b = lax.ppermute(from_up[n:], "group", _y_shift(size, -1))
    out = jnp.zeros((Y_PARTS * 2 * n,) + h.shape[1:], h.dtype)
    for dy, piece in ((0, pair), (-1, from_down), (1, from_up),
                      (2, jnp.concatenate([far_a, far_b]))):
        out = lax.dynamic_update_slice_in_dim(out, piece, ((y + dy) % Y_PARTS) * 2 * n, 0)
    return out


def on_device(tokens, proj_in, proj_out, expert_list, block_pattern, route_weight):
    group_size = lax.axis_size("group")
    n_dp = lax.axis_size("dp")
    dp_index = lax.axis_index("dp")
    row_count, width_here = tokens.shape
    slots = expert_list.shape[1]
    ff_here = proj_in.shape[1]
    block_rows = row_count // block_pattern.shape[2]

    own_pattern = lax.dynamic_index_in_dim(block_pattern, dp_index, 0, keepdims=False)
    block_mask = jnp.repeat(own_pattern, block_rows, axis=1).astype(jnp.float32)
    token_scale = route_weight.T * block_mask

    send_in = jnp.take(proj_in, expert_list, axis=0).transpose(0, 1, 3, 2, 4)
    send_out = jnp.take(proj_out, expert_list, axis=0)

    gathered = []
    weights_out = []
    pending = tokens
    for slot in range(slots):
        pending, piece = lax.optimization_barrier((pending, send_in[:, slot]))
        weight_in = lax.all_to_all(piece, "dp", 0, 0, tiled=True).reshape(-1, width_here)
        partial_here = jnp.dot(weight_in, tokens.T, preferred_element_type=jnp.float32)
        partial_here = partial_here.astype(jnp.bfloat16)
        shares = group_reduce_scatter(partial_here)
        gathered.append(shares)
        pending = partial_here
    for slot in range(slots):
        pending, piece = lax.optimization_barrier((pending, send_out[:, slot]))
        weight_out = lax.all_to_all(piece, "dp", 0, 0, tiled=True)
        weights_out.append(weight_out.reshape(-1, width_here))
        pending = weight_out

    combined = None
    for slot in range(slots):
        shares = gathered[slot].reshape(n_dp // group_size, 2, ff_here, row_count)
        hidden = (token_scale[slot] * jax.nn.silu(shares[:, 0]) * shares[:, 1]).astype(jnp.bfloat16)
        hidden = group_all_gather(hidden.reshape(-1, row_count))
        term = lax.dot_general(
            hidden, weights_out[slot], (((0,), (0,)), ((), ())), preferred_element_type=jnp.float32
        )
        combined = term if combined is None else combined + term
    return combined.astype(jnp.bfloat16)


def solution(mesh):
    return jax.shard_map(
        on_device,
        mesh=mesh,
        in_specs=(
            P("dp", "group"),
            P(None, "dp", None, "group"),
            P(None, "dp", "group"),
            P(),
            P(),
            P("dp", None),
        ),
        out_specs=P("dp", "group"),
        check_vma=False,
    )
```

```python
import jax
import jax.numpy as jnp
from jax import lax
from jax.sharding import PartitionSpec as P


Y_PARTS = 4


def _perm(size, fn):
    return [(j, fn(j)) for j in range(size)]


def _y_shift(size, dy):
    z_parts = size // Y_PARTS
    return _perm(size, lambda j: ((j // z_parts + dy) % Y_PARTS) * z_parts + j % z_parts)


def _z_flip(size):
    return _perm(size, lambda j: j ^ 1)


def group_reduce_scatter(x):
    size = lax.axis_size("group")
    j = lax.axis_index("group")
    y, zh = j // 2, j % 2
    rows = x.shape[0] // Y_PARTS
    half = rows // 2

    def block(yy):
        return lax.dynamic_slice_in_dim(x, (yy % Y_PARTS) * rows, rows, 0)

    far = block(y + 2)
    up = lax.ppermute(block(y + 1), "group", _y_shift(size, 1))
    down = lax.ppermute(block(y - 1), "group", _y_shift(size, -1))
    up_far = lax.ppermute(far[:half], "group", _y_shift(size, 1))
    down_far = lax.ppermute(far[half:], "group", _y_shift(size, -1))
    relay_up = lax.ppermute(up_far, "group", _y_shift(size, 1))
    relay_down = lax.ppermute(down_far, "group", _y_shift(size, -1))
    f32 = jnp.float32
    y_sum = (
        block(y).astype(f32) + up.astype(f32) + down.astype(f32)
        + jnp.concatenate([relay_up, relay_down], axis=0).astype(f32)
    )
    mine = lax.dynamic_slice_in_dim(y_sum, zh * half, half, 0)
    other = lax.dynamic_slice_in_dim(y_sum, (1 - zh) * half, half, 0)
    return mine + lax.ppermute(other.astype(jnp.bfloat16), "group", _z_flip(size)).astype(f32)


def group_all_gather(h):
    size = lax.axis_size("group")
    j = lax.axis_index("group")
    y, zh = j // 2, j % 2
    n = h.shape[0]
    partner = lax.ppermute(h, "group", _z_flip(size))
    pair = jnp.where(zh == 0, jnp.concatenate([h, partner]), jnp.concatenate([partner, h]))
    from_down = lax.ppermute(pair, "group", _y_shift(size, 1))
    from_up = lax.ppermute(pair, "group", _y_shift(size, -1))
    far_a = lax.ppermute(from_down[:n], "group", _y_shift(size, 1))
    far_b = lax.ppermute(from_up[n:], "group", _y_shift(size, -1))
    out = jnp.zeros((Y_PARTS * 2 * n,) + h.shape[1:], h.dtype)
    for dy, piece in ((0, pair), (-1, from_down), (1, from_up),
                      (2, jnp.concatenate([far_a, far_b]))):
        out = lax.dynamic_update_slice_in_dim(out, piece, ((y + dy) % Y_PARTS) * 2 * n, 0)
    return out


def on_device(tokens, proj_in, proj_out, expert_list, block_pattern, route_weight):
    group_size = lax.axis_size("group")
    n_dp = lax.axis_size("dp")
    dp_index = lax.axis_index("dp")
    row_count, width_here = tokens.shape
    slots = expert_list.shape[1]
    ff_here = proj_in.shape[1]
    block_rows = row_count // block_pattern.shape[2]

    own_pattern = lax.dynamic_index_in_dim(block_pattern, dp_index, 0, keepdims=False)
    block_mask = jnp.repeat(own_pattern, block_rows, axis=1).astype(jnp.float32)
    token_scale = route_weight.T * block_mask

    send_in = jnp.take(proj_in, expert_list, axis=0, mode="clip").transpose(0, 1, 3, 2, 4)
    send_out = jnp.take(proj_out, expert_list, axis=0, mode="clip")

    hiddens = []
    weights_out = []
    pending = tokens
    for slot in range(slots):
        pending, piece = lax.optimization_barrier((pending, send_in[:, slot]))
        weight_in = lax.all_to_all(piece, "dp", 0, 0, tiled=True).reshape(-1, width_here)
        if hiddens:
            weight_in, hiddens[-1] = lax.optimization_barrier((weight_in, hiddens[-1]))
        partial_here = jnp.dot(weight_in, tokens.T, preferred_element_type=jnp.float32)
        partial_here = partial_here.astype(jnp.bfloat16)
        shares = group_reduce_scatter(partial_here)
        shares = shares.reshape(n_dp // group_size, 2, ff_here, row_count)
        hidden = (token_scale[slot] * jax.nn.silu(shares[:, 0]) * shares[:, 1]).astype(jnp.bfloat16)
        hiddens.append(group_all_gather(hidden.reshape(-1, row_count)))
        pending = partial_here
    for slot in range(slots):
        pending, piece = lax.optimization_barrier((pending, send_out[:, slot]))
        weight_out = lax.all_to_all(piece, "dp", 0, 0, tiled=True)
        weights_out.append(weight_out.reshape(-1, width_here))
        pending = weight_out

    combined = None
    for slot in range(slots):
        term = lax.dot_general(
            hiddens[slot], weights_out[slot], (((0,), (0,)), ((), ())),
            preferred_element_type=jnp.float32,
        )
        combined = term if combined is None else combined + term
    return combined.astype(jnp.bfloat16)


def solution(mesh):
    return jax.shard_map(
        on_device,
        mesh=mesh,
        in_specs=(
            P("dp", "group"),
            P(None, "dp", None, "group"),
            P(None, "dp", "group"),
            P(),
            P(),
            P("dp", None),
        ),
        out_specs=P("dp", "group"),
        check_vma=False,
    )
```

```python
import jax
import jax.numpy as jnp
from jax import lax
from jax.experimental import pallas as pl
from jax.experimental.pallas import tpu as pltpu
from jax.sharding import PartitionSpec as P


Y_PARTS = 4


def _perm(size, fn):
    return [(j, fn(j)) for j in range(size)]


def _y_shift(size, dy):
    z_parts = size // Y_PARTS
    return _perm(size, lambda j: ((j // z_parts + dy) % Y_PARTS) * z_parts + j % z_parts)


def _z_flip(size):
    return _perm(size, lambda j: j ^ 1)


def _rs_kernel(x_ref, out_ref, ybuf, own, zsend, zrecv, send_sem, recv_sem, local_sem):
    size = lax.axis_size("group")
    z_parts = size // Y_PARTS
    j = lax.axis_index("group")
    y, zh = j // z_parts, j % z_parts
    rows = x_ref.shape[0] // Y_PARTS
    half = rows // 2

    def peer(dy):
        return ((y + dy) % Y_PARTS) * z_parts + zh

    partner = y * z_parts + (1 - zh)
    shifts = (1, Y_PARTS - 1, 2)
    barrier = pltpu.get_barrier_semaphore()
    for dy in shifts:
        pl.semaphore_signal(barrier, inc=1, device_id={"group": peer(dy)},
                            device_id_type=pl.DeviceIdType.MESH)
    pl.semaphore_signal(barrier, inc=1, device_id={"group": partner},
                        device_id_type=pl.DeviceIdType.MESH)
    pl.semaphore_wait(barrier, len(shifts) + 1)

    copies = []
    for k, dy in enumerate(shifts):
        start = pl.multiple_of(((y + dy) % Y_PARTS) * rows, rows)
        c = pltpu.make_async_remote_copy(
            src_ref=x_ref.at[pl.ds(start, rows)],
            dst_ref=ybuf.at[k],
            send_sem=send_sem.at[k],
            recv_sem=recv_sem.at[k],
            device_id={"group": peer(dy)},
            device_id_type=pl.DeviceIdType.MESH,
        )
        c.start()
        copies.append(c)
    mine_start = pl.multiple_of(y * rows, rows)
    local = pltpu.make_async_copy(x_ref.at[pl.ds(mine_start, rows)], own, local_sem.at[0])
    local.start()
    local.wait()
    for c in copies:
        c.wait()

    f32 = jnp.float32

    def y_sum(lo):
        sl = pl.ds(lo, half)
        total = own[sl, :].astype(f32)
        for k in range(len(shifts)):
            total = total + ybuf[k, sl, :].astype(f32)
        return total

    other_lo = pl.multiple_of((1 - zh) * half, half)
    mine_lo = pl.multiple_of(zh * half, half)
    zsend[...] = y_sum(other_lo).astype(zsend.dtype)
    zc = pltpu.make_async_remote_copy(
        src_ref=zsend, dst_ref=zrecv, send_sem=send_sem.at[3], recv_sem=recv_sem.at[3],
        device_id={"group": partner}, device_id_type=pl.DeviceIdType.MESH,
    )
    zc.start()
    out_ref[...] = y_sum(mine_lo)
    zc.wait()
    out_ref[...] += zrecv[...].astype(f32)


def group_reduce_scatter(x, collective_id=0):
    size = lax.axis_size("group")
    r, c = x.shape
    rows = r // Y_PARTS
    half = rows // 2
    return pl.pallas_call(
        _rs_kernel,
        out_shape=jax.ShapeDtypeStruct((r // size, c), jnp.float32),
        in_specs=[pl.BlockSpec(memory_space=pl.ANY)],
        out_specs=pl.BlockSpec(memory_space=pltpu.VMEM),
        scratch_shapes=[
            pltpu.VMEM((3, rows, c), x.dtype),
            pltpu.VMEM((rows, c), x.dtype),
            pltpu.VMEM((half, c), x.dtype),
            pltpu.VMEM((half, c), x.dtype),
            pltpu.SemaphoreType.DMA((4,)),
            pltpu.SemaphoreType.DMA((4,)),
            pltpu.SemaphoreType.DMA((1,)),
        ],
        compiler_params=pltpu.CompilerParams(
            collective_id=collective_id, has_side_effects=True, vmem_limit_bytes=48 * 1024 * 1024
        ),
    )(x)


def group_all_gather(h):
    size = lax.axis_size("group")
    j = lax.axis_index("group")
    y, zh = j // 2, j % 2
    n = h.shape[0]
    partner = lax.ppermute(h, "group", _z_flip(size))
    pair = jnp.where(zh == 0, jnp.concatenate([h, partner]), jnp.concatenate([partner, h]))
    from_down = lax.ppermute(pair, "group", _y_shift(size, 1))
    from_up = lax.ppermute(pair, "group", _y_shift(size, -1))
    far_a = lax.ppermute(from_down[:n], "group", _y_shift(size, 1))
    far_b = lax.ppermute(from_up[n:], "group", _y_shift(size, -1))
    out = jnp.zeros((Y_PARTS * 2 * n,) + h.shape[1:], h.dtype)
    for dy, piece in ((0, pair), (-1, from_down), (1, from_up),
                      (2, jnp.concatenate([far_a, far_b]))):
        out = lax.dynamic_update_slice_in_dim(out, piece, ((y + dy) % Y_PARTS) * 2 * n, 0)
    return out


def on_device(tokens, proj_in, proj_out, expert_list, block_pattern, route_weight):
    group_size = lax.axis_size("group")
    n_dp = lax.axis_size("dp")
    dp_index = lax.axis_index("dp")
    row_count, width_here = tokens.shape
    slots = expert_list.shape[1]
    ff_here = proj_in.shape[1]
    block_rows = row_count // block_pattern.shape[2]

    own_pattern = lax.dynamic_index_in_dim(block_pattern, dp_index, 0, keepdims=False)
    block_mask = jnp.repeat(own_pattern, block_rows, axis=1).astype(jnp.float32)
    token_scale = route_weight.T * block_mask

    send_in = jnp.take(proj_in, expert_list, axis=0, mode="clip").transpose(0, 1, 3, 2, 4)
    send_out = jnp.take(proj_out, expert_list, axis=0, mode="clip")

    hiddens = []
    weights_out = []
    pending = tokens
    for slot in range(slots):
        pending, piece = lax.optimization_barrier((pending, send_in[:, slot]))
        weight_in = lax.all_to_all(piece, "dp", 0, 0, tiled=True).reshape(-1, width_here)
        if hiddens:
            weight_in, hiddens[-1] = lax.optimization_barrier((weight_in, hiddens[-1]))
        partial_here = jnp.dot(weight_in, tokens.T, preferred_element_type=jnp.float32)
        partial_here = partial_here.astype(jnp.bfloat16)
        shares = group_reduce_scatter(partial_here, collective_id=slot)
        shares = shares.reshape(n_dp // group_size, 2, ff_here, row_count)
        hidden = (token_scale[slot] * jax.nn.silu(shares[:, 0]) * shares[:, 1]).astype(jnp.bfloat16)
        hiddens.append(group_all_gather(hidden.reshape(-1, row_count)))
        pending = partial_here
    for slot in range(slots):
        pending, piece = lax.optimization_barrier((pending, send_out[:, slot]))
        weight_out = lax.all_to_all(piece, "dp", 0, 0, tiled=True)
        weights_out.append(weight_out.reshape(-1, width_here))
        pending = weight_out

    combined = None
    for slot in range(slots):
        term = lax.dot_general(
            hiddens[slot], weights_out[slot], (((0,), (0,)), ((), ())),
            preferred_element_type=jnp.float32,
        )
        combined = term if combined is None else combined + term
    return combined.astype(jnp.bfloat16)


def solution(mesh):
    return jax.shard_map(
        on_device,
        mesh=mesh,
        in_specs=(
            P("dp", "group"),
            P(None, "dp", None, "group"),
            P(None, "dp", "group"),
            P(),
            P(),
            P("dp", None),
        ),
        out_specs=P("dp", "group"),
        check_vma=False,
    )
```

```python
import jax
import jax.numpy as jnp
from jax import lax
from jax.experimental import pallas as pl
from jax.experimental.pallas import tpu as pltpu
from jax.sharding import PartitionSpec as P


Y_PARTS = 4


def _perm(size, fn):
    return [(j, fn(j)) for j in range(size)]


def _y_shift(size, dy):
    z_parts = size // Y_PARTS
    return _perm(size, lambda j: ((j // z_parts + dy) % Y_PARTS) * z_parts + j % z_parts)


def _z_flip(size):
    return _perm(size, lambda j: j ^ 1)


def _rs_kernel(x_ref, out_ref, ybuf, own, zsend, zrecv, send_sem, recv_sem, local_sem):
    size = lax.axis_size("group")
    z_parts = size // Y_PARTS
    j = lax.axis_index("group")
    y, zh = j // z_parts, j % z_parts
    rows = x_ref.shape[0] // Y_PARTS
    half = rows // 2

    def peer(dy):
        return ((y + dy) % Y_PARTS) * z_parts + zh

    partner = y * z_parts + (1 - zh)
    shifts = (1, Y_PARTS - 1, 2)
    barrier = pltpu.get_barrier_semaphore()
    for dy in shifts:
        pl.semaphore_signal(barrier, inc=1, device_id={"group": peer(dy)},
                            device_id_type=pl.DeviceIdType.MESH)
    pl.semaphore_signal(barrier, inc=1, device_id={"group": partner},
                        device_id_type=pl.DeviceIdType.MESH)
    pl.semaphore_wait(barrier, len(shifts) + 1)

    copies = []
    for k, dy in enumerate(shifts):
        start = pl.multiple_of(((y + dy) % Y_PARTS) * rows, rows)
        c = pltpu.make_async_remote_copy(
            src_ref=x_ref.at[pl.ds(start, rows)],
            dst_ref=ybuf.at[k],
            send_sem=send_sem.at[k],
            recv_sem=recv_sem.at[k],
            device_id={"group": peer(dy)},
            device_id_type=pl.DeviceIdType.MESH,
        )
        c.start()
        copies.append(c)
    mine_start = pl.multiple_of(y * rows, rows)
    local = pltpu.make_async_copy(x_ref.at[pl.ds(mine_start, rows)], own, local_sem.at[0])
    local.start()
    local.wait()
    for c in copies:
        c.wait()

    f32 = jnp.float32

    def y_sum(lo):
        sl = pl.ds(lo, half)
        total = own[sl, :].astype(f32)
        for k in range(len(shifts)):
            total = total + ybuf[k, sl, :].astype(f32)
        return total

    other_lo = pl.multiple_of((1 - zh) * half, half)
    mine_lo = pl.multiple_of(zh * half, half)
    zsend[...] = y_sum(other_lo).astype(zsend.dtype)
    zc = pltpu.make_async_remote_copy(
        src_ref=zsend, dst_ref=zrecv, send_sem=send_sem.at[3], recv_sem=recv_sem.at[3],
        device_id={"group": partner}, device_id_type=pl.DeviceIdType.MESH,
    )
    zc.start()
    out_ref[...] = y_sum(mine_lo)
    zc.wait()
    out_ref[...] += zrecv[...].astype(f32)


def group_reduce_scatter(x, collective_id=0):
    size = lax.axis_size("group")
    r, c = x.shape
    rows = r // Y_PARTS
    half = rows // 2
    return pl.pallas_call(
        _rs_kernel,
        out_shape=jax.ShapeDtypeStruct((r // size, c), jnp.float32),
        in_specs=[pl.BlockSpec(memory_space=pl.ANY)],
        out_specs=pl.BlockSpec(memory_space=pltpu.VMEM),
        scratch_shapes=[
            pltpu.VMEM((3, rows, c), x.dtype),
            pltpu.VMEM((rows, c), x.dtype),
            pltpu.VMEM((half, c), x.dtype),
            pltpu.VMEM((half, c), x.dtype),
            pltpu.SemaphoreType.DMA((4,)),
            pltpu.SemaphoreType.DMA((4,)),
            pltpu.SemaphoreType.DMA((1,)),
        ],
        compiler_params=pltpu.CompilerParams(
            collective_id=collective_id, has_side_effects=True, vmem_limit_bytes=48 * 1024 * 1024
        ),
    )(x)


def group_all_gather(h):
    size = lax.axis_size("group")
    j = lax.axis_index("group")
    y, zh = j // 2, j % 2
    n = h.shape[0]
    partner = lax.ppermute(h, "group", _z_flip(size))
    pair = jnp.where(zh == 0, jnp.concatenate([h, partner]), jnp.concatenate([partner, h]))
    from_down = lax.ppermute(pair, "group", _y_shift(size, 1))
    from_up = lax.ppermute(pair, "group", _y_shift(size, -1))
    far_a = lax.ppermute(from_down[:n], "group", _y_shift(size, 1))
    far_b = lax.ppermute(from_up[n:], "group", _y_shift(size, -1))
    out = jnp.zeros((Y_PARTS * 2 * n,) + h.shape[1:], h.dtype)
    for dy, piece in ((0, pair), (-1, from_down), (1, from_up),
                      (2, jnp.concatenate([far_a, far_b]))):
        out = lax.dynamic_update_slice_in_dim(out, piece, ((y + dy) % Y_PARTS) * 2 * n, 0)
    return out


def on_device(tokens, proj_in, proj_out, expert_list, block_pattern, route_weight):
    group_size = lax.axis_size("group")
    n_dp = lax.axis_size("dp")
    dp_index = lax.axis_index("dp")
    row_count, width_here = tokens.shape
    slots = expert_list.shape[1]
    ff_here = proj_in.shape[1]
    block_rows = row_count // block_pattern.shape[2]

    own_pattern = lax.dynamic_index_in_dim(block_pattern, dp_index, 0, keepdims=False)
    block_mask = jnp.repeat(own_pattern, block_rows, axis=1).astype(jnp.float32)
    token_scale = route_weight.T * block_mask

    send_out = jnp.take(proj_out, expert_list, axis=0, mode="clip")

    hiddens = []
    pending = tokens
    for slot in range(slots):
        piece = jnp.take(proj_in, expert_list[:, slot], axis=0, mode="clip").transpose(0, 2, 1, 3)
        pending, piece = lax.optimization_barrier((pending, piece))
        weight_in = lax.all_to_all(piece, "dp", 0, 0, tiled=True).reshape(-1, width_here)
        if hiddens:
            weight_in, hiddens[-1] = lax.optimization_barrier((weight_in, hiddens[-1]))
        partial_here = jnp.dot(weight_in, tokens.T, preferred_element_type=jnp.float32)
        partial_here = partial_here.astype(jnp.bfloat16)
        shares = group_reduce_scatter(partial_here, collective_id=slot)
        shares = shares.reshape(n_dp // group_size, 2, ff_here, row_count)
        hidden = (token_scale[slot] * jax.nn.silu(shares[:, 0]) * shares[:, 1]).astype(jnp.bfloat16)
        hiddens.append(group_all_gather(hidden.reshape(-1, row_count)))
        pending = partial_here
    pending, send_out = lax.optimization_barrier((pending, send_out))
    weights_out = lax.all_to_all(send_out, "dp", 0, 0, tiled=True)

    combined = None
    for slot in range(slots):
        term = lax.dot_general(
            hiddens[slot], weights_out[:, slot].reshape(-1, width_here), (((0,), (0,)), ((), ())),
            preferred_element_type=jnp.float32,
        )
        combined = term if combined is None else combined + term
    return combined.astype(jnp.bfloat16)


def solution(mesh):
    return jax.shard_map(
        on_device,
        mesh=mesh,
        in_specs=(
            P("dp", "group"),
            P(None, "dp", None, "group"),
            P(None, "dp", "group"),
            P(),
            P(),
            P("dp", None),
        ),
        out_specs=P("dp", "group"),
        check_vma=False,
    )
```

```python
import jax
import jax.numpy as jnp
from jax import lax
from jax.experimental import pallas as pl
from jax.experimental.pallas import tpu as pltpu
from jax.sharding import PartitionSpec as P


Y_PARTS = 4


def _perm(size, fn):
    return [(j, fn(j)) for j in range(size)]


def _y_shift(size, dy):
    z_parts = size // Y_PARTS
    return _perm(size, lambda j: ((j // z_parts + dy) % Y_PARTS) * z_parts + j % z_parts)


def _z_flip(size):
    return _perm(size, lambda j: j ^ 1)


def _rs_kernel(x_ref, out_ref, ybuf, fwd, relay, own, zsend, zrecv, send_sem, recv_sem, local_sem):
    size = lax.axis_size("group")
    z_parts = size // Y_PARTS
    j = lax.axis_index("group")
    y, zh = j // z_parts, j % z_parts
    rows = x_ref.shape[0] // Y_PARTS
    half = rows // 2
    mesh_id = pl.DeviceIdType.MESH

    def peer(dy):
        return {"group": ((y + dy) % Y_PARTS) * z_parts + zh}

    def block_at(dy):
        return pl.multiple_of(((y + dy) % Y_PARTS) * rows, rows)

    partner = {"group": y * z_parts + (1 - zh)}
    up, down = peer(1), peer(Y_PARTS - 1)
    barrier = pltpu.get_barrier_semaphore()
    for dev in (up, down, partner):
        pl.semaphore_signal(barrier, inc=1, device_id=dev, device_id_type=mesh_id)
    pl.semaphore_wait(barrier, 3)

    def remote(src, dst, k, dev):
        c = pltpu.make_async_remote_copy(
            src_ref=src, dst_ref=dst, send_sem=send_sem.at[k], recv_sem=recv_sem.at[k],
            device_id=dev, device_id_type=mesh_id,
        )
        c.start()
        return c

    far = block_at(2)
    first = [
        remote(x_ref.at[pl.ds(block_at(1), rows)], ybuf.at[0], 0, up),
        remote(x_ref.at[pl.ds(block_at(-1), rows)], ybuf.at[1], 1, down),
        remote(x_ref.at[pl.ds(far, half)], fwd.at[0], 2, up),
        remote(x_ref.at[pl.ds(far + half, half)], fwd.at[1], 3, down),
    ]
    local = pltpu.make_async_copy(x_ref.at[pl.ds(block_at(0), rows)], own, local_sem.at[0])
    local.start()
    for c in first:
        c.wait()
    second = [
        remote(fwd.at[0], relay.at[pl.ds(0, half)], 4, up),
        remote(fwd.at[1], relay.at[pl.ds(half, half)], 5, down),
    ]
    local.wait()

    f32 = jnp.float32

    def near_sum(lo):
        sl = pl.ds(lo, half)
        return own[sl, :].astype(f32) + ybuf[0, sl, :].astype(f32) + ybuf[1, sl, :].astype(f32)

    other_lo = pl.multiple_of((1 - zh) * half, half)
    mine_lo = pl.multiple_of(zh * half, half)
    out_ref[...] = near_sum(other_lo)
    for c in second:
        c.wait()
    zsend[...] = (out_ref[...] + relay[pl.ds(other_lo, half), :].astype(f32)).astype(zsend.dtype)
    zc = remote(zsend, zrecv, 6, partner)
    out_ref[...] = near_sum(mine_lo) + relay[pl.ds(mine_lo, half), :].astype(f32)
    zc.wait()
    out_ref[...] += zrecv[...].astype(f32)


def group_reduce_scatter(x, collective_id=0):
    size = lax.axis_size("group")
    r, c = x.shape
    rows = r // Y_PARTS
    half = rows // 2
    return pl.pallas_call(
        _rs_kernel,
        out_shape=jax.ShapeDtypeStruct((r // size, c), jnp.float32),
        in_specs=[pl.BlockSpec(memory_space=pl.ANY)],
        out_specs=pl.BlockSpec(memory_space=pltpu.VMEM),
        scratch_shapes=[
            pltpu.VMEM((2, rows, c), x.dtype),
            pltpu.VMEM((2, half, c), x.dtype),
            pltpu.VMEM((rows, c), x.dtype),
            pltpu.VMEM((rows, c), x.dtype),
            pltpu.VMEM((half, c), x.dtype),
            pltpu.VMEM((half, c), x.dtype),
            pltpu.SemaphoreType.DMA((7,)),
            pltpu.SemaphoreType.DMA((7,)),
            pltpu.SemaphoreType.DMA((1,)),
        ],
        compiler_params=pltpu.CompilerParams(
            collective_id=collective_id, has_side_effects=True, vmem_limit_bytes=48 * 1024 * 1024
        ),
    )(x)


def group_all_gather(h):
    size = lax.axis_size("group")
    j = lax.axis_index("group")
    y, zh = j // 2, j % 2
    n = h.shape[0]
    partner = lax.ppermute(h, "group", _z_flip(size))
    pair = jnp.where(zh == 0, jnp.concatenate([h, partner]), jnp.concatenate([partner, h]))
    from_down = lax.ppermute(pair, "group", _y_shift(size, 1))
    from_up = lax.ppermute(pair, "group", _y_shift(size, -1))
    far_a = lax.ppermute(from_down[:n], "group", _y_shift(size, 1))
    far_b = lax.ppermute(from_up[n:], "group", _y_shift(size, -1))
    out = jnp.zeros((Y_PARTS * 2 * n,) + h.shape[1:], h.dtype)
    for dy, piece in ((0, pair), (-1, from_down), (1, from_up),
                      (2, jnp.concatenate([far_a, far_b]))):
        out = lax.dynamic_update_slice_in_dim(out, piece, ((y + dy) % Y_PARTS) * 2 * n, 0)
    return out


def on_device(tokens, proj_in, proj_out, expert_list, block_pattern, route_weight):
    group_size = lax.axis_size("group")
    n_dp = lax.axis_size("dp")
    dp_index = lax.axis_index("dp")
    row_count, width_here = tokens.shape
    slots = expert_list.shape[1]
    ff_here = proj_in.shape[1]
    block_rows = row_count // block_pattern.shape[2]

    own_pattern = lax.dynamic_index_in_dim(block_pattern, dp_index, 0, keepdims=False)
    block_mask = jnp.repeat(own_pattern, block_rows, axis=1).astype(jnp.float32)
    token_scale = route_weight.T * block_mask

    send_out = jnp.take(proj_out, expert_list, axis=0, mode="clip")

    hiddens = []
    pending = tokens
    for slot in range(slots):
        piece = jnp.take(proj_in, expert_list[:, slot], axis=0, mode="clip").transpose(0, 2, 1, 3)
        pending, piece = lax.optimization_barrier((pending, piece))
        weight_in = lax.all_to_all(piece, "dp", 0, 0, tiled=True).reshape(-1, width_here)
        if hiddens:
            weight_in, hiddens[-1] = lax.optimization_barrier((weight_in, hiddens[-1]))
        partial_here = jnp.dot(weight_in, tokens.T, preferred_element_type=jnp.float32)
        partial_here = partial_here.astype(jnp.bfloat16)
        shares = group_reduce_scatter(partial_here, collective_id=slot)
        shares = shares.reshape(n_dp // group_size, 2, ff_here, row_count)
        hidden = (token_scale[slot] * jax.nn.silu(shares[:, 0]) * shares[:, 1]).astype(jnp.bfloat16)
        hiddens.append(group_all_gather(hidden.reshape(-1, row_count)))
        pending = partial_here
    pending, send_out = lax.optimization_barrier((pending, send_out))
    weights_out = lax.all_to_all(send_out, "dp", 0, 0, tiled=True)

    combined = None
    for slot in range(slots):
        term = lax.dot_general(
            hiddens[slot], weights_out[:, slot].reshape(-1, width_here), (((0,), (0,)), ((), ())),
            preferred_element_type=jnp.float32,
        )
        combined = term if combined is None else combined + term
    return combined.astype(jnp.bfloat16)


def solution(mesh):
    return jax.shard_map(
        on_device,
        mesh=mesh,
        in_specs=(
            P("dp", "group"),
            P(None, "dp", None, "group"),
            P(None, "dp", "group"),
            P(),
            P(),
            P("dp", None),
        ),
        out_specs=P("dp", "group"),
        check_vma=False,
    )
```

```python
import jax
import jax.numpy as jnp
from jax import lax
from jax.experimental import pallas as pl
from jax.experimental.pallas import tpu as pltpu
from jax.sharding import PartitionSpec as P


Y_PARTS = 4


def _perm(size, fn):
    return [(j, fn(j)) for j in range(size)]


def _y_shift(size, dy):
    z_parts = size // Y_PARTS
    return _perm(size, lambda j: ((j // z_parts + dy) % Y_PARTS) * z_parts + j % z_parts)


def _z_flip(size):
    return _perm(size, lambda j: j ^ 1)


def _rs_kernel(x_ref, out_ref, ybuf, fwd, relay, own, zsend, zrecv, send_sem, recv_sem, local_sem):
    size = lax.axis_size("group")
    z_parts = size // Y_PARTS
    j = lax.axis_index("group")
    y, zh = j // z_parts, j % z_parts
    rows = x_ref.shape[0] // Y_PARTS
    half = rows // 2
    mesh_id = pl.DeviceIdType.MESH

    def peer(dy):
        return {"group": ((y + dy) % Y_PARTS) * z_parts + zh}

    def block_at(dy):
        return pl.multiple_of(((y + dy) % Y_PARTS) * rows, rows)

    partner = {"group": y * z_parts + (1 - zh)}
    up, down = peer(1), peer(Y_PARTS - 1)
    barrier = pltpu.get_barrier_semaphore()
    for dev in (up, down, partner):
        pl.semaphore_signal(barrier, inc=1, device_id=dev, device_id_type=mesh_id)
    pl.semaphore_wait(barrier, 3)

    def remote(src, dst, k, dev):
        c = pltpu.make_async_remote_copy(
            src_ref=src, dst_ref=dst, send_sem=send_sem.at[k], recv_sem=recv_sem.at[k],
            device_id=dev, device_id_type=mesh_id,
        )
        c.start()
        return c

    far = block_at(2)
    first = [
        remote(x_ref.at[pl.ds(block_at(1), rows)], ybuf.at[0], 0, up),
        remote(x_ref.at[pl.ds(block_at(-1), rows)], ybuf.at[1], 1, down),
        remote(x_ref.at[pl.ds(far, half)], fwd.at[0], 2, up),
        remote(x_ref.at[pl.ds(far + half, half)], fwd.at[1], 3, down),
    ]
    local = pltpu.make_async_copy(x_ref.at[pl.ds(block_at(0), rows)], own, local_sem.at[0])
    local.start()
    for c in first:
        c.wait()
    second = [
        remote(fwd.at[0], relay.at[pl.ds(0, half)], 4, up),
        remote(fwd.at[1], relay.at[pl.ds(half, half)], 5, down),
    ]
    local.wait()

    f32 = jnp.float32

    def near_sum(lo):
        sl = pl.ds(lo, half)
        return own[sl, :].astype(f32) + ybuf[0, sl, :].astype(f32) + ybuf[1, sl, :].astype(f32)

    other_lo = pl.multiple_of((1 - zh) * half, half)
    mine_lo = pl.multiple_of(zh * half, half)
    out_ref[...] = near_sum(other_lo)
    for c in second:
        c.wait()
    zsend[...] = (out_ref[...] + relay[pl.ds(other_lo, half), :].astype(f32)).astype(zsend.dtype)
    zc = remote(zsend, zrecv, 6, partner)
    out_ref[...] = near_sum(mine_lo) + relay[pl.ds(mine_lo, half), :].astype(f32)
    zc.wait()
    out_ref[...] += zrecv[...].astype(f32)


def group_reduce_scatter(x, collective_id=0):
    size = lax.axis_size("group")
    r, c = x.shape
    rows = r // Y_PARTS
    half = rows // 2
    return pl.pallas_call(
        _rs_kernel,
        out_shape=jax.ShapeDtypeStruct((r // size, c), jnp.float32),
        in_specs=[pl.BlockSpec(memory_space=pl.ANY)],
        out_specs=pl.BlockSpec(memory_space=pltpu.VMEM),
        scratch_shapes=[
            pltpu.VMEM((2, rows, c), x.dtype),
            pltpu.VMEM((2, half, c), x.dtype),
            pltpu.VMEM((rows, c), x.dtype),
            pltpu.VMEM((rows, c), x.dtype),
            pltpu.VMEM((half, c), x.dtype),
            pltpu.VMEM((half, c), x.dtype),
            pltpu.SemaphoreType.DMA((7,)),
            pltpu.SemaphoreType.DMA((7,)),
            pltpu.SemaphoreType.DMA((1,)),
        ],
        compiler_params=pltpu.CompilerParams(
            collective_id=collective_id, has_side_effects=True, vmem_limit_bytes=48 * 1024 * 1024
        ),
    )(x)


def group_all_gather(h):
    size = lax.axis_size("group")
    j = lax.axis_index("group")
    y, zh = j // 2, j % 2
    n = h.shape[0]
    partner = lax.ppermute(h, "group", _z_flip(size))
    pair = jnp.where(zh == 0, jnp.concatenate([h, partner]), jnp.concatenate([partner, h]))
    from_down = lax.ppermute(pair, "group", _y_shift(size, 1))
    from_up = lax.ppermute(pair, "group", _y_shift(size, -1))
    far_a = lax.ppermute(from_down[:n], "group", _y_shift(size, 1))
    far_b = lax.ppermute(from_up[n:], "group", _y_shift(size, -1))
    out = jnp.zeros((Y_PARTS * 2 * n,) + h.shape[1:], h.dtype)
    for dy, piece in ((0, pair), (-1, from_down), (1, from_up),
                      (2, jnp.concatenate([far_a, far_b]))):
        out = lax.dynamic_update_slice_in_dim(out, piece, ((y + dy) % Y_PARTS) * 2 * n, 0)
    return out


def on_device(tokens, proj_in, proj_out, expert_list, block_pattern, route_weight):
    group_size = lax.axis_size("group")
    n_dp = lax.axis_size("dp")
    dp_index = lax.axis_index("dp")
    row_count, width_here = tokens.shape
    slots = expert_list.shape[1]
    ff_here = proj_in.shape[1]
    block_rows = row_count // block_pattern.shape[2]

    own_pattern = lax.dynamic_index_in_dim(block_pattern, dp_index, 0, keepdims=False)
    block_mask = jnp.repeat(own_pattern, block_rows, axis=1).astype(jnp.float32)
    token_scale = route_weight.T * block_mask

    send_out = jnp.take(proj_out, expert_list, axis=0, mode="clip")

    hiddens = []
    pending = tokens
    for slot in range(slots):
        piece = jnp.take(proj_in, expert_list[:, slot], axis=0, mode="clip").transpose(0, 2, 1, 3)
        pending, piece = lax.optimization_barrier((pending, piece))
        weight_in = lax.all_to_all(piece, "dp", 0, 0, tiled=True).reshape(-1, width_here)
        if hiddens:
            weight_in, hiddens[-1] = lax.optimization_barrier((weight_in, hiddens[-1]))
        partial_here = jnp.dot(weight_in, tokens.T, preferred_element_type=jnp.float32)
        partial_here = partial_here.astype(jnp.bfloat16)
        shares = group_reduce_scatter(partial_here, collective_id=slot)
        shares = shares.reshape(n_dp // group_size, 2, ff_here, row_count)
        hidden = (token_scale[slot] * jax.nn.silu(shares[:, 0]) * shares[:, 1]).astype(jnp.bfloat16)
        hiddens.append(hidden.reshape(-1, row_count))
        pending = partial_here
    pending, send_out = lax.optimization_barrier((pending, send_out))
    weights_out = lax.all_to_all(send_out, "dp", 0, 0, tiled=True)

    hidden_all = group_all_gather(jnp.concatenate(hiddens, axis=0))
    hidden_all = hidden_all.reshape(group_size, slots, n_dp // group_size, ff_here, row_count)
    weights_out = weights_out.reshape(group_size, n_dp // group_size, slots, ff_here, width_here)
    combined = lax.dot_general(
        hidden_all, weights_out, (((0, 1, 2, 3), (0, 2, 1, 3)), ((), ())),
        preferred_element_type=jnp.float32,
    )
    return combined.astype(jnp.bfloat16)


def solution(mesh):
    return jax.shard_map(
        on_device,
        mesh=mesh,
        in_specs=(
            P("dp", "group"),
            P(None, "dp", None, "group"),
            P(None, "dp", "group"),
            P(),
            P(),
            P("dp", None),
        ),
        out_specs=P("dp", "group"),
        check_vma=False,
    )
```

```python
import jax
import jax.numpy as jnp
from jax import lax
from jax.experimental import pallas as pl
from jax.experimental.pallas import tpu as pltpu
from jax.sharding import PartitionSpec as P


Y_PARTS = 4


def _perm(size, fn):
    return [(j, fn(j)) for j in range(size)]


def _y_shift(size, dy):
    z_parts = size // Y_PARTS
    return _perm(size, lambda j: ((j // z_parts + dy) % Y_PARTS) * z_parts + j % z_parts)


def _z_flip(size):
    return _perm(size, lambda j: j ^ 1)


def _rs_kernel(x_ref, out_ref, ybuf, fwd, relay, own, zsend, zrecv, send_sem, recv_sem, local_sem):
    size = lax.axis_size("group")
    z_parts = size // Y_PARTS
    j = lax.axis_index("group")
    y, zh = j // z_parts, j % z_parts
    rows = x_ref.shape[0] // Y_PARTS
    half = rows // 2
    mesh_id = pl.DeviceIdType.MESH

    def peer(dy):
        return {"group": ((y + dy) % Y_PARTS) * z_parts + zh}

    def block_at(dy):
        return pl.multiple_of(((y + dy) % Y_PARTS) * rows, rows)

    partner = {"group": y * z_parts + (1 - zh)}
    up, down = peer(1), peer(Y_PARTS - 1)
    barrier = pltpu.get_barrier_semaphore()
    for dev in (up, down, partner):
        pl.semaphore_signal(barrier, inc=1, device_id=dev, device_id_type=mesh_id)
    pl.semaphore_wait(barrier, 3)

    def remote(src, dst, k, dev):
        c = pltpu.make_async_remote_copy(
            src_ref=src, dst_ref=dst, send_sem=send_sem.at[k], recv_sem=recv_sem.at[k],
            device_id=dev, device_id_type=mesh_id,
        )
        c.start()
        return c

    far = block_at(2)
    first = [
        remote(x_ref.at[pl.ds(block_at(1), rows)], ybuf.at[0], 0, up),
        remote(x_ref.at[pl.ds(block_at(-1), rows)], ybuf.at[1], 1, down),
        remote(x_ref.at[pl.ds(far, half)], fwd.at[0], 2, up),
        remote(x_ref.at[pl.ds(far + half, half)], fwd.at[1], 3, down),
    ]
    local = pltpu.make_async_copy(x_ref.at[pl.ds(block_at(0), rows)], own, local_sem.at[0])
    local.start()
    for c in first:
        c.wait()
    second = [
        remote(fwd.at[0], relay.at[pl.ds(0, half)], 4, up),
        remote(fwd.at[1], relay.at[pl.ds(half, half)], 5, down),
    ]
    local.wait()

    f32 = jnp.float32

    def near_sum(lo):
        sl = pl.ds(lo, half)
        return own[sl, :].astype(f32) + ybuf[0, sl, :].astype(f32) + ybuf[1, sl, :].astype(f32)

    other_lo = pl.multiple_of((1 - zh) * half, half)
    mine_lo = pl.multiple_of(zh * half, half)
    out_ref[...] = near_sum(other_lo)
    for c in second:
        c.wait()
    zsend[...] = (out_ref[...] + relay[pl.ds(other_lo, half), :].astype(f32)).astype(zsend.dtype)
    zc = remote(zsend, zrecv, 6, partner)
    out_ref[...] = near_sum(mine_lo) + relay[pl.ds(mine_lo, half), :].astype(f32)
    zc.wait()
    out_ref[...] += zrecv[...].astype(f32)


def group_reduce_scatter(x, collective_id=0):
    size = lax.axis_size("group")
    r, c = x.shape
    rows = r // Y_PARTS
    half = rows // 2
    return pl.pallas_call(
        _rs_kernel,
        out_shape=jax.ShapeDtypeStruct((r // size, c), jnp.float32),
        in_specs=[pl.BlockSpec(memory_space=pl.ANY)],
        out_specs=pl.BlockSpec(memory_space=pltpu.VMEM),
        scratch_shapes=[
            pltpu.VMEM((2, rows, c), x.dtype),
            pltpu.VMEM((2, half, c), x.dtype),
            pltpu.VMEM((rows, c), x.dtype),
            pltpu.VMEM((rows, c), x.dtype),
            pltpu.VMEM((half, c), x.dtype),
            pltpu.VMEM((half, c), x.dtype),
            pltpu.SemaphoreType.DMA((7,)),
            pltpu.SemaphoreType.DMA((7,)),
            pltpu.SemaphoreType.DMA((1,)),
        ],
        compiler_params=pltpu.CompilerParams(
            collective_id=collective_id, has_side_effects=True, vmem_limit_bytes=48 * 1024 * 1024
        ),
    )(x)


def group_all_gather(h):
    size = lax.axis_size("group")
    j = lax.axis_index("group")
    y, zh = j // 2, j % 2
    n = h.shape[0]
    partner = lax.ppermute(h, "group", _z_flip(size))
    pair = jnp.where(zh == 0, jnp.concatenate([h, partner]), jnp.concatenate([partner, h]))
    from_down = lax.ppermute(pair, "group", _y_shift(size, 1))
    from_up = lax.ppermute(pair, "group", _y_shift(size, -1))
    far_a = lax.ppermute(from_down[:n], "group", _y_shift(size, 1))
    far_b = lax.ppermute(from_up[n:], "group", _y_shift(size, -1))
    out = jnp.zeros((Y_PARTS * 2 * n,) + h.shape[1:], h.dtype)
    for dy, piece in ((0, pair), (-1, from_down), (1, from_up),
                      (2, jnp.concatenate([far_a, far_b]))):
        out = lax.dynamic_update_slice_in_dim(out, piece, ((y + dy) % Y_PARTS) * 2 * n, 0)
    return out


def on_device(tokens, proj_in, proj_out, expert_list, block_pattern, route_weight):
    group_size = lax.axis_size("group")
    n_dp = lax.axis_size("dp")
    dp_index = lax.axis_index("dp")
    row_count, width_here = tokens.shape
    slots = expert_list.shape[1]
    ff_here = proj_in.shape[1]
    block_rows = row_count // block_pattern.shape[2]

    own_pattern = lax.dynamic_index_in_dim(block_pattern, dp_index, 0, keepdims=False)
    block_mask = jnp.repeat(own_pattern, block_rows, axis=1).astype(jnp.float32)
    token_scale = route_weight.T * block_mask

    send_out = jnp.take(proj_out, expert_list, axis=0, mode="clip")

    weights_in = []
    for slot in range(slots):
        piece = jnp.take(proj_in, expert_list[:, slot], axis=0, mode="clip").transpose(0, 2, 1, 3)
        weights_in.append(lax.all_to_all(piece, "dp", 0, 0, tiled=True).reshape(-1, width_here))
    weights_out = lax.all_to_all(send_out, "dp", 0, 0, tiled=True)

    hiddens = []
    for slot in range(slots):
        weight_in = weights_in[slot]
        if hiddens:
            weight_in, hiddens[-1] = lax.optimization_barrier((weight_in, hiddens[-1]))
        partial_here = jnp.dot(weight_in, tokens.T, preferred_element_type=jnp.float32)
        partial_here = partial_here.astype(jnp.bfloat16)
        shares = group_reduce_scatter(partial_here, collective_id=slot)
        shares = shares.reshape(n_dp // group_size, 2, ff_here, row_count)
        hidden = (token_scale[slot] * jax.nn.silu(shares[:, 0]) * shares[:, 1]).astype(jnp.bfloat16)
        hiddens.append(hidden.reshape(-1, row_count))

    hidden_all = group_all_gather(jnp.concatenate(hiddens, axis=0))
    hidden_all = hidden_all.reshape(group_size, slots, n_dp // group_size, ff_here, row_count)
    weights_out = weights_out.reshape(group_size, n_dp // group_size, slots, ff_here, width_here)
    combined = lax.dot_general(
        hidden_all, weights_out, (((0, 1, 2, 3), (0, 2, 1, 3)), ((), ())),
        preferred_element_type=jnp.float32,
    )
    return combined.astype(jnp.bfloat16)


def solution(mesh):
    return jax.shard_map(
        on_device,
        mesh=mesh,
        in_specs=(
            P("dp", "group"),
            P(None, "dp", None, "group"),
            P(None, "dp", "group"),
            P(),
            P(),
            P("dp", None),
        ),
        out_specs=P("dp", "group"),
        check_vma=False,
    )
```

```python
import jax
import jax.numpy as jnp
from jax import lax
from jax.experimental import pallas as pl
from jax.experimental.pallas import tpu as pltpu
from jax.sharding import PartitionSpec as P


Y_PARTS = 4
COL_PARTS = 2


def _perm(size, fn):
    return [(j, fn(j)) for j in range(size)]


def _y_shift(size, dy):
    z_parts = size // Y_PARTS
    return _perm(size, lambda j: ((j // z_parts + dy) % Y_PARTS) * z_parts + j % z_parts)


def _z_flip(size):
    return _perm(size, lambda j: j ^ 1)


def _rs_kernel(x_ref, out_ref, ybuf, fwd, relay, own, zsend, zrecv, send_sem, recv_sem, local_sem):
    size = lax.axis_size("group")
    z_parts = size // Y_PARTS
    j = lax.axis_index("group")
    y, zh = j // z_parts, j % z_parts
    rows = x_ref.shape[0] // Y_PARTS
    half = rows // 2
    width = x_ref.shape[1] // COL_PARTS
    mesh_id = pl.DeviceIdType.MESH
    f32 = jnp.float32

    def peer(dy):
        return {"group": ((y + dy) % Y_PARTS) * z_parts + zh}

    def block_at(dy):
        return pl.multiple_of(((y + dy) % Y_PARTS) * rows, rows)

    partner = {"group": y * z_parts + (1 - zh)}
    up, down = peer(1), peer(Y_PARTS - 1)
    barrier = pltpu.get_barrier_semaphore()
    for dev in (up, down, partner):
        pl.semaphore_signal(barrier, inc=1, device_id=dev, device_id_type=mesh_id)
    pl.semaphore_wait(barrier, 3)

    def remote(src, dst, p, k, dev):
        c = pltpu.make_async_remote_copy(
            src_ref=src, dst_ref=dst, send_sem=send_sem.at[p, k], recv_sem=recv_sem.at[p, k],
            device_id=dev, device_id_type=mesh_id,
        )
        c.start()
        return c

    far = block_at(2)
    other_lo = pl.multiple_of((1 - zh) * half, half)
    mine_lo = pl.multiple_of(zh * half, half)

    def first_round(p):
        cols = pl.ds(p * width, width)
        copies = [
            remote(x_ref.at[pl.ds(block_at(1), rows), cols], ybuf.at[p, 0], p, 0, up),
            remote(x_ref.at[pl.ds(block_at(-1), rows), cols], ybuf.at[p, 1], p, 1, down),
            remote(x_ref.at[pl.ds(far, half), cols], fwd.at[p, 0], p, 2, up),
            remote(x_ref.at[pl.ds(far + half, half), cols], fwd.at[p, 1], p, 3, down),
        ]
        local = pltpu.make_async_copy(
            x_ref.at[pl.ds(block_at(0), rows), cols], own.at[p], local_sem.at[p])
        local.start()
        return copies, local

    def near_sum(p, lo):
        sl = pl.ds(lo, half)
        return (own[p, sl, :].astype(f32) + ybuf[p, 0, sl, :].astype(f32)
                + ybuf[p, 1, sl, :].astype(f32))

    pending = first_round(0)
    z_copies = []
    for p in range(COL_PARTS):
        copies, local = pending
        for c in copies:
            c.wait()
        second = [
            remote(fwd.at[p, 0], relay.at[p, pl.ds(0, half)], p, 4, up),
            remote(fwd.at[p, 1], relay.at[p, pl.ds(half, half)], p, 5, down),
        ]
        if p + 1 < COL_PARTS:
            pending = first_round(p + 1)
        local.wait()
        cols = pl.ds(p * width, width)
        out_ref[:, cols] = near_sum(p, other_lo)
        for c in second:
            c.wait()
        zsend[p] = (out_ref[:, cols] + relay[p, pl.ds(other_lo, half), :].astype(f32)).astype(zsend.dtype)
        z_copies.append(remote(zsend.at[p], zrecv.at[p], p, 6, partner))
        out_ref[:, cols] = near_sum(p, mine_lo) + relay[p, pl.ds(mine_lo, half), :].astype(f32)
    for p, zc in enumerate(z_copies):
        zc.wait()
        cols = pl.ds(p * width, width)
        out_ref[:, cols] += zrecv[p].astype(f32)


def group_reduce_scatter(x, collective_id=0):
    size = lax.axis_size("group")
    r, c = x.shape
    rows = r // Y_PARTS
    half = rows // 2
    width = c // COL_PARTS
    return pl.pallas_call(
        _rs_kernel,
        out_shape=jax.ShapeDtypeStruct((r // size, c), jnp.float32),
        in_specs=[pl.BlockSpec(memory_space=pl.ANY)],
        out_specs=pl.BlockSpec(memory_space=pltpu.VMEM),
        scratch_shapes=[
            pltpu.VMEM((COL_PARTS, 2, rows, width), x.dtype),
            pltpu.VMEM((COL_PARTS, 2, half, width), x.dtype),
            pltpu.VMEM((COL_PARTS, rows, width), x.dtype),
            pltpu.VMEM((COL_PARTS, rows, width), x.dtype),
            pltpu.VMEM((COL_PARTS, half, width), x.dtype),
            pltpu.VMEM((COL_PARTS, half, width), x.dtype),
            pltpu.SemaphoreType.DMA((COL_PARTS, 7)),
            pltpu.SemaphoreType.DMA((COL_PARTS, 7)),
            pltpu.SemaphoreType.DMA((COL_PARTS,)),
        ],
        compiler_params=pltpu.CompilerParams(
            collective_id=collective_id, has_side_effects=True, vmem_limit_bytes=48 * 1024 * 1024
        ),
    )(x)


def group_all_gather(h):
    size = lax.axis_size("group")
    j = lax.axis_index("group")
    y, zh = j // 2, j % 2
    n = h.shape[0]
    partner = lax.ppermute(h, "group", _z_flip(size))
    pair = jnp.where(zh == 0, jnp.concatenate([h, partner]), jnp.concatenate([partner, h]))
    from_down = lax.ppermute(pair, "group", _y_shift(size, 1))
    from_up = lax.ppermute(pair, "group", _y_shift(size, -1))
    far_a = lax.ppermute(from_down[:n], "group", _y_shift(size, 1))
    far_b = lax.ppermute(from_up[n:], "group", _y_shift(size, -1))
    out = jnp.zeros((Y_PARTS * 2 * n,) + h.shape[1:], h.dtype)
    for dy, piece in ((0, pair), (-1, from_down), (1, from_up),
                      (2, jnp.concatenate([far_a, far_b]))):
        out = lax.dynamic_update_slice_in_dim(out, piece, ((y + dy) % Y_PARTS) * 2 * n, 0)
    return out


def on_device(tokens, proj_in, proj_out, expert_list, block_pattern, route_weight):
    group_size = lax.axis_size("group")
    n_dp = lax.axis_size("dp")
    dp_index = lax.axis_index("dp")
    row_count, width_here = tokens.shape
    slots = expert_list.shape[1]
    ff_here = proj_in.shape[1]
    block_rows = row_count // block_pattern.shape[2]

    own_pattern = lax.dynamic_index_in_dim(block_pattern, dp_index, 0, keepdims=False)
    block_mask = jnp.repeat(own_pattern, block_rows, axis=1).astype(jnp.float32)
    token_scale = route_weight.T * block_mask

    send_out = jnp.take(proj_out, expert_list, axis=0, mode="clip")

    hiddens = []
    pending = tokens
    for slot in range(slots):
        piece = jnp.take(proj_in, expert_list[:, slot], axis=0, mode="clip").transpose(0, 2, 1, 3)
        pending, piece = lax.optimization_barrier((pending, piece))
        weight_in = lax.all_to_all(piece, "dp", 0, 0, tiled=True).reshape(-1, width_here)
        if hiddens:
            weight_in, hiddens[-1] = lax.optimization_barrier((weight_in, hiddens[-1]))
        partial_here = jnp.dot(weight_in, tokens.T, preferred_element_type=jnp.float32)
        partial_here = partial_here.astype(jnp.bfloat16)
        shares = group_reduce_scatter(partial_here, collective_id=slot)
        shares = shares.reshape(n_dp // group_size, 2, ff_here, row_count)
        hidden = (token_scale[slot] * jax.nn.silu(shares[:, 0]) * shares[:, 1]).astype(jnp.bfloat16)
        hiddens.append(group_all_gather(hidden.reshape(-1, row_count)))
        pending = partial_here
    pending, send_out = lax.optimization_barrier((pending, send_out))
    weights_out = lax.all_to_all(send_out, "dp", 0, 0, tiled=True)

    combined = None
    for slot in range(slots):
        term = lax.dot_general(
            hiddens[slot], weights_out[:, slot].reshape(-1, width_here), (((0,), (0,)), ((), ())),
            preferred_element_type=jnp.float32,
        )
        combined = term if combined is None else combined + term
    return combined.astype(jnp.bfloat16)


def solution(mesh):
    return jax.shard_map(
        on_device,
        mesh=mesh,
        in_specs=(
            P("dp", "group"),
            P(None, "dp", None, "group"),
            P(None, "dp", "group"),
            P(),
            P(),
            P("dp", None),
        ),
        out_specs=P("dp", "group"),
        check_vma=False,
    )
```

```python
import jax
import jax.numpy as jnp
from jax import lax
from jax.experimental import pallas as pl
from jax.experimental.pallas import tpu as pltpu
from jax.sharding import PartitionSpec as P


Y_PARTS = 4


def _rs_kernel(x_ref, out_ref, ybuf, fwd, relay, own, zsend, zrecv, send_sem, recv_sem, local_sem):
    size = lax.axis_size("group")
    z_parts = size // Y_PARTS
    j = lax.axis_index("group")
    y, zh = j // z_parts, j % z_parts
    rows = x_ref.shape[0] // Y_PARTS
    half = rows // 2
    mesh_id = pl.DeviceIdType.MESH

    def peer(dy):
        return {"group": ((y + dy) % Y_PARTS) * z_parts + zh}

    def block_at(dy):
        return pl.multiple_of(((y + dy) % Y_PARTS) * rows, rows)

    partner = {"group": y * z_parts + (1 - zh)}
    up, down = peer(1), peer(Y_PARTS - 1)
    barrier = pltpu.get_barrier_semaphore()
    for dev in (up, down, partner):
        pl.semaphore_signal(barrier, inc=1, device_id=dev, device_id_type=mesh_id)
    pl.semaphore_wait(barrier, 3)

    def remote(src, dst, k, dev):
        c = pltpu.make_async_remote_copy(
            src_ref=src, dst_ref=dst, send_sem=send_sem.at[k], recv_sem=recv_sem.at[k],
            device_id=dev, device_id_type=mesh_id,
        )
        c.start()
        return c

    far = block_at(2)
    first = [
        remote(x_ref.at[pl.ds(block_at(1), rows)], ybuf.at[0], 0, up),
        remote(x_ref.at[pl.ds(block_at(-1), rows)], ybuf.at[1], 1, down),
        remote(x_ref.at[pl.ds(far, half)], fwd.at[0], 2, up),
        remote(x_ref.at[pl.ds(far + half, half)], fwd.at[1], 3, down),
    ]
    local = pltpu.make_async_copy(x_ref.at[pl.ds(block_at(0), rows)], own, local_sem.at[0])
    local.start()
    for c in first:
        c.wait()
    second = [
        remote(fwd.at[0], relay.at[pl.ds(0, half)], 4, up),
        remote(fwd.at[1], relay.at[pl.ds(half, half)], 5, down),
    ]
    local.wait()

    f32 = jnp.float32

    def near_sum(lo):
        sl = pl.ds(lo, half)
        return own[sl, :].astype(f32) + ybuf[0, sl, :].astype(f32) + ybuf[1, sl, :].astype(f32)

    other_lo = pl.multiple_of((1 - zh) * half, half)
    mine_lo = pl.multiple_of(zh * half, half)
    out_ref[...] = near_sum(other_lo)
    for c in second:
        c.wait()
    zsend[...] = (out_ref[...] + relay[pl.ds(other_lo, half), :].astype(f32)).astype(zsend.dtype)
    zc = remote(zsend, zrecv, 6, partner)
    out_ref[...] = near_sum(mine_lo) + relay[pl.ds(mine_lo, half), :].astype(f32)
    zc.wait()
    out_ref[...] += zrecv[...].astype(f32)


def group_reduce_scatter(x, collective_id=0):
    size = lax.axis_size("group")
    r, c = x.shape
    rows = r // Y_PARTS
    half = rows // 2
    return pl.pallas_call(
        _rs_kernel,
        out_shape=jax.ShapeDtypeStruct((r // size, c), jnp.float32),
        in_specs=[pl.BlockSpec(memory_space=pl.ANY)],
        out_specs=pl.BlockSpec(memory_space=pltpu.VMEM),
        scratch_shapes=[
            pltpu.VMEM((2, rows, c), x.dtype),
            pltpu.VMEM((2, half, c), x.dtype),
            pltpu.VMEM((rows, c), x.dtype),
            pltpu.VMEM((rows, c), x.dtype),
            pltpu.VMEM((half, c), x.dtype),
            pltpu.VMEM((half, c), x.dtype),
            pltpu.SemaphoreType.DMA((7,)),
            pltpu.SemaphoreType.DMA((7,)),
            pltpu.SemaphoreType.DMA((1,)),
        ],
        compiler_params=pltpu.CompilerParams(
            collective_id=collective_id, has_side_effects=True, vmem_limit_bytes=48 * 1024 * 1024
        ),
    )(x)


def _ag_kernel(h_ref, out_ref, pbuf, ybuf, fbuf, send_sem, recv_sem):
    size = lax.axis_size("group")
    z_parts = size // Y_PARTS
    j = lax.axis_index("group")
    y, zh = j // z_parts, j % z_parts
    n = h_ref.shape[0]
    mesh_id = pl.DeviceIdType.MESH

    def peer(dy):
        return {"group": ((y + dy) % Y_PARTS) * z_parts + zh}

    partner = {"group": y * z_parts + (1 - zh)}
    up, down = peer(1), peer(Y_PARTS - 1)
    barrier = pltpu.get_barrier_semaphore()
    for dev in (up, down, partner):
        pl.semaphore_signal(barrier, inc=1, device_id=dev, device_id_type=mesh_id)
    pl.semaphore_wait(barrier, 3)

    def remote(src, dst, k, dev):
        c = pltpu.make_async_remote_copy(
            src_ref=src, dst_ref=dst, send_sem=send_sem.at[k], recv_sem=recv_sem.at[k],
            device_id=dev, device_id_type=mesh_id,
        )
        c.start()
        return c

    own_lo = pl.multiple_of(zh * n, n)
    other_lo = pl.multiple_of((1 - zh) * n, n)
    zc = remote(h_ref, pbuf, 0, partner)
    first = [
        remote(h_ref, ybuf.at[0, pl.ds(own_lo, n)], 1, up),
        remote(h_ref, ybuf.at[1, pl.ds(own_lo, n)], 2, down),
    ]
    zc.wait()
    first += [
        remote(pbuf, ybuf.at[0, pl.ds(other_lo, n)], 3, up),
        remote(pbuf, ybuf.at[1, pl.ds(other_lo, n)], 4, down),
    ]
    for c in first:
        c.wait()
    second = [
        remote(ybuf.at[0, pl.ds(0, n)], fbuf.at[0], 5, up),
        remote(ybuf.at[1, pl.ds(n, n)], fbuf.at[1], 6, down),
    ]
    pair = 2 * n

    def at(dy):
        return pl.multiple_of(((y + dy) % Y_PARTS) * pair, pair)

    out_ref[pl.ds(at(0) + own_lo, n), :] = h_ref[...]
    out_ref[pl.ds(at(0) + other_lo, n), :] = pbuf[...]
    out_ref[pl.ds(at(-1), pair), :] = ybuf[0]
    out_ref[pl.ds(at(1), pair), :] = ybuf[1]
    for c in second:
        c.wait()
    out_ref[pl.ds(at(2), n), :] = fbuf[0]
    out_ref[pl.ds(at(2) + n, n), :] = fbuf[1]


def group_all_gather(h, collective_id=0):
    size = lax.axis_size("group")
    n, c = h.shape
    return pl.pallas_call(
        _ag_kernel,
        out_shape=jax.ShapeDtypeStruct((size * n, c), h.dtype),
        in_specs=[pl.BlockSpec(memory_space=pltpu.VMEM)],
        out_specs=pl.BlockSpec(memory_space=pltpu.VMEM),
        scratch_shapes=[
            pltpu.VMEM((n, c), h.dtype),
            pltpu.VMEM((2, 2 * n, c), h.dtype),
            pltpu.VMEM((2, n, c), h.dtype),
            pltpu.SemaphoreType.DMA((7,)),
            pltpu.SemaphoreType.DMA((7,)),
        ],
        compiler_params=pltpu.CompilerParams(
            collective_id=collective_id, has_side_effects=True, vmem_limit_bytes=32 * 1024 * 1024
        ),
    )(h)


def on_device(tokens, proj_in, proj_out, expert_list, block_pattern, route_weight):
    group_size = lax.axis_size("group")
    n_dp = lax.axis_size("dp")
    dp_index = lax.axis_index("dp")
    row_count, width_here = tokens.shape
    slots = expert_list.shape[1]
    ff_here = proj_in.shape[1]
    block_rows = row_count // block_pattern.shape[2]

    own_pattern = lax.dynamic_index_in_dim(block_pattern, dp_index, 0, keepdims=False)
    block_mask = jnp.repeat(own_pattern, block_rows, axis=1).astype(jnp.float32)
    token_scale = route_weight.T * block_mask

    send_out = jnp.take(proj_out, expert_list, axis=0, mode="clip")

    hiddens = []
    pending = tokens
    for slot in range(slots):
        piece = jnp.take(proj_in, expert_list[:, slot], axis=0, mode="clip").transpose(0, 2, 1, 3)
        pending, piece = lax.optimization_barrier((pending, piece))
        weight_in = lax.all_to_all(piece, "dp", 0, 0, tiled=True).reshape(-1, width_here)
        if hiddens:
            weight_in, hiddens[-1] = lax.optimization_barrier((weight_in, hiddens[-1]))
        partial_here = jnp.dot(weight_in, tokens.T, preferred_element_type=jnp.float32)
        partial_here = partial_here.astype(jnp.bfloat16)
        shares = group_reduce_scatter(partial_here, collective_id=slot)
        shares = shares.reshape(n_dp // group_size, 2, ff_here, row_count)
        hidden = (token_scale[slot] * jax.nn.silu(shares[:, 0]) * shares[:, 1]).astype(jnp.bfloat16)
        hiddens.append(group_all_gather(hidden.reshape(-1, row_count), collective_id=slots + slot))
        pending = partial_here
    pending, send_out = lax.optimization_barrier((pending, send_out))
    weights_out = lax.all_to_all(send_out, "dp", 0, 0, tiled=True)

    combined = None
    for slot in range(slots):
        term = lax.dot_general(
            hiddens[slot], weights_out[:, slot].reshape(-1, width_here), (((0,), (0,)), ((), ())),
            preferred_element_type=jnp.float32,
        )
        combined = term if combined is None else combined + term
    return combined.astype(jnp.bfloat16)


def solution(mesh):
    return jax.shard_map(
        on_device,
        mesh=mesh,
        in_specs=(
            P("dp", "group"),
            P(None, "dp", None, "group"),
            P(None, "dp", "group"),
            P(),
            P(),
            P("dp", None),
        ),
        out_specs=P("dp", "group"),
        check_vma=False,
    )
```

```python
import jax
import jax.numpy as jnp
from jax import lax
from jax.experimental import pallas as pl
from jax.experimental.pallas import tpu as pltpu
from jax.sharding import PartitionSpec as P


Y_PARTS = 4


def _rs_kernel(x_ref, out_ref, ybuf, fwd, relay, own, zsend, zrecv, send_sem, recv_sem, local_sem):
    size = lax.axis_size("group")
    z_parts = size // Y_PARTS
    j = lax.axis_index("group")
    y, zh = j // z_parts, j % z_parts
    rows = x_ref.shape[0] // Y_PARTS
    half = rows // 2
    mesh_id = pl.DeviceIdType.MESH

    def peer(dy):
        return {"group": ((y + dy) % Y_PARTS) * z_parts + zh}

    def block_at(dy):
        return pl.multiple_of(((y + dy) % Y_PARTS) * rows, rows)

    partner = {"group": y * z_parts + (1 - zh)}
    up, down = peer(1), peer(Y_PARTS - 1)
    barrier = pltpu.get_barrier_semaphore()
    for dev in (up, down, partner):
        pl.semaphore_signal(barrier, inc=1, device_id=dev, device_id_type=mesh_id)
    pl.semaphore_wait(barrier, 3)

    def remote(src, dst, k, dev):
        c = pltpu.make_async_remote_copy(
            src_ref=src, dst_ref=dst, send_sem=send_sem.at[k], recv_sem=recv_sem.at[k],
            device_id=dev, device_id_type=mesh_id,
        )
        c.start()
        return c

    far = block_at(2)
    first = [
        remote(x_ref.at[pl.ds(block_at(1), rows)], ybuf.at[0], 0, up),
        remote(x_ref.at[pl.ds(block_at(-1), rows)], ybuf.at[1], 1, down),
        remote(x_ref.at[pl.ds(far, half)], fwd.at[0], 2, up),
        remote(x_ref.at[pl.ds(far + half, half)], fwd.at[1], 3, down),
    ]
    local = pltpu.make_async_copy(x_ref.at[pl.ds(block_at(0), rows)], own, local_sem.at[0])
    local.start()
    for c in first:
        c.wait()
    second = [
        remote(fwd.at[0], relay.at[pl.ds(0, half)], 4, up),
        remote(fwd.at[1], relay.at[pl.ds(half, half)], 5, down),
    ]
    local.wait()

    f32 = jnp.float32

    def near_sum(lo):
        sl = pl.ds(lo, half)
        return own[sl, :].astype(f32) + ybuf[0, sl, :].astype(f32) + ybuf[1, sl, :].astype(f32)

    other_lo = pl.multiple_of((1 - zh) * half, half)
    mine_lo = pl.multiple_of(zh * half, half)
    out_ref[...] = near_sum(other_lo)
    for c in second:
        c.wait()
    zsend[...] = (out_ref[...] + relay[pl.ds(other_lo, half), :].astype(f32)).astype(zsend.dtype)
    zc = remote(zsend, zrecv, 6, partner)
    out_ref[...] = near_sum(mine_lo) + relay[pl.ds(mine_lo, half), :].astype(f32)
    zc.wait()
    out_ref[...] += zrecv[...].astype(f32)


def group_reduce_scatter(x, collective_id=0):
    size = lax.axis_size("group")
    r, c = x.shape
    rows = r // Y_PARTS
    half = rows // 2
    return pl.pallas_call(
        _rs_kernel,
        out_shape=jax.ShapeDtypeStruct((r // size, c), jnp.float32),
        in_specs=[pl.BlockSpec(memory_space=pl.ANY)],
        out_specs=pl.BlockSpec(memory_space=pltpu.VMEM),
        scratch_shapes=[
            pltpu.VMEM((2, rows, c), x.dtype),
            pltpu.VMEM((2, half, c), x.dtype),
            pltpu.VMEM((rows, c), x.dtype),
            pltpu.VMEM((rows, c), x.dtype),
            pltpu.VMEM((half, c), x.dtype),
            pltpu.VMEM((half, c), x.dtype),
            pltpu.SemaphoreType.DMA((7,)),
            pltpu.SemaphoreType.DMA((7,)),
            pltpu.SemaphoreType.DMA((1,)),
        ],
        compiler_params=pltpu.CompilerParams(
            collective_id=collective_id, has_side_effects=True, vmem_limit_bytes=48 * 1024 * 1024
        ),
    )(x)


def _ag_kernel(h_ref, out_ref, pbuf, ybuf, fbuf, send_sem, recv_sem):
    size = lax.axis_size("group")
    z_parts = size // Y_PARTS
    j = lax.axis_index("group")
    y, zh = j // z_parts, j % z_parts
    n = h_ref.shape[0]
    mesh_id = pl.DeviceIdType.MESH

    def peer(dy):
        return {"group": ((y + dy) % Y_PARTS) * z_parts + zh}

    partner = {"group": y * z_parts + (1 - zh)}
    up, down = peer(1), peer(Y_PARTS - 1)
    barrier = pltpu.get_barrier_semaphore()
    for dev in (up, down, partner):
        pl.semaphore_signal(barrier, inc=1, device_id=dev, device_id_type=mesh_id)
    pl.semaphore_wait(barrier, 3)

    def remote(src, dst, k, dev):
        c = pltpu.make_async_remote_copy(
            src_ref=src, dst_ref=dst, send_sem=send_sem.at[k], recv_sem=recv_sem.at[k],
            device_id=dev, device_id_type=mesh_id,
        )
        c.start()
        return c

    own_lo = pl.multiple_of(zh * n, n)
    other_lo = pl.multiple_of((1 - zh) * n, n)
    zc = remote(h_ref, pbuf, 0, partner)
    first = [
        remote(h_ref, ybuf.at[0, pl.ds(own_lo, n)], 1, up),
        remote(h_ref, ybuf.at[1, pl.ds(own_lo, n)], 2, down),
    ]
    zc.wait()
    first += [
        remote(pbuf, ybuf.at[0, pl.ds(other_lo, n)], 3, up),
        remote(pbuf, ybuf.at[1, pl.ds(other_lo, n)], 4, down),
    ]
    for c in first:
        c.wait()
    second = [
        remote(ybuf.at[0, pl.ds(0, n)], fbuf.at[0], 5, up),
        remote(ybuf.at[1, pl.ds(n, n)], fbuf.at[1], 6, down),
    ]
    pair = 2 * n

    def at(dy):
        return pl.multiple_of(((y + dy) % Y_PARTS) * pair, pair)

    out_ref[pl.ds(at(0) + own_lo, n), :] = h_ref[...]
    out_ref[pl.ds(at(0) + other_lo, n), :] = pbuf[...]
    out_ref[pl.ds(at(-1), pair), :] = ybuf[0]
    out_ref[pl.ds(at(1), pair), :] = ybuf[1]
    for c in second:
        c.wait()
    out_ref[pl.ds(at(2), n), :] = fbuf[0]
    out_ref[pl.ds(at(2) + n, n), :] = fbuf[1]


def group_all_gather(h, collective_id=0):
    size = lax.axis_size("group")
    n, c = h.shape
    return pl.pallas_call(
        _ag_kernel,
        out_shape=jax.ShapeDtypeStruct((size * n, c), h.dtype),
        in_specs=[pl.BlockSpec(memory_space=pltpu.VMEM)],
        out_specs=pl.BlockSpec(memory_space=pltpu.VMEM),
        scratch_shapes=[
            pltpu.VMEM((n, c), h.dtype),
            pltpu.VMEM((2, 2 * n, c), h.dtype),
            pltpu.VMEM((2, n, c), h.dtype),
            pltpu.SemaphoreType.DMA((7,)),
            pltpu.SemaphoreType.DMA((7,)),
        ],
        compiler_params=pltpu.CompilerParams(
            collective_id=collective_id, has_side_effects=True, vmem_limit_bytes=32 * 1024 * 1024
        ),
    )(h)


def on_device(tokens, proj_in, proj_out, expert_list, block_pattern, route_weight):
    group_size = lax.axis_size("group")
    n_dp = lax.axis_size("dp")
    dp_index = lax.axis_index("dp")
    row_count, width_here = tokens.shape
    slots = expert_list.shape[1]
    ff_here = proj_in.shape[1]
    block_rows = row_count // block_pattern.shape[2]

    own_pattern = lax.dynamic_index_in_dim(block_pattern, dp_index, 0, keepdims=False)
    block_mask = jnp.repeat(own_pattern, block_rows, axis=1).astype(jnp.float32)
    token_scale = route_weight.T * block_mask

    send_out = jnp.take(proj_out, expert_list, axis=0, mode="clip")

    hiddens = []
    pending = tokens
    for slot in range(slots):
        piece = jnp.take(proj_in, expert_list[:, slot], axis=0, mode="clip")
        pending, piece = lax.optimization_barrier((pending, piece))
        weight_in = lax.all_to_all(piece, "dp", 0, 0, tiled=True).reshape(-1, width_here)
        if hiddens:
            weight_in, hiddens[-1] = lax.optimization_barrier((weight_in, hiddens[-1]))
        partial_here = jnp.dot(weight_in, tokens.T, preferred_element_type=jnp.float32)
        partial_here = partial_here.astype(jnp.bfloat16)
        shares = group_reduce_scatter(partial_here, collective_id=slot)
        shares = shares.reshape(n_dp // group_size, ff_here, 2, row_count)
        hidden = (token_scale[slot] * jax.nn.silu(shares[:, :, 0]) * shares[:, :, 1]).astype(jnp.bfloat16)
        hiddens.append(group_all_gather(hidden.reshape(-1, row_count), collective_id=slots + slot))
        pending = partial_here
    pending, send_out = lax.optimization_barrier((pending, send_out))
    weights_out = lax.all_to_all(send_out, "dp", 0, 0, tiled=True)

    combined = None
    for slot in range(slots):
        term = lax.dot_general(
            hiddens[slot], weights_out[:, slot].reshape(-1, width_here), (((0,), (0,)), ((), ())),
            preferred_element_type=jnp.float32,
        )
        combined = term if combined is None else combined + term
    return combined.astype(jnp.bfloat16)


def solution(mesh):
    return jax.shard_map(
        on_device,
        mesh=mesh,
        in_specs=(
            P("dp", "group"),
            P(None, "dp", None, "group"),
            P(None, "dp", "group"),
            P(),
            P(),
            P("dp", None),
        ),
        out_specs=P("dp", "group"),
        check_vma=False,
    )
```

```python
import jax
import jax.numpy as jnp
from jax import lax
from jax.experimental import pallas as pl
from jax.experimental.pallas import tpu as pltpu
from jax.sharding import PartitionSpec as P


Y_PARTS = 4


def _rs_kernel(x_ref, out_ref, ybuf, fwd, relay, own, zsend, zrecv, send_sem, recv_sem, local_sem):
    size = lax.axis_size("group")
    z_parts = size // Y_PARTS
    j = lax.axis_index("group")
    y, zh = j // z_parts, j % z_parts
    rows = x_ref.shape[0] // Y_PARTS
    half = rows // 2
    mesh_id = pl.DeviceIdType.MESH

    def peer(dy):
        return {"group": ((y + dy) % Y_PARTS) * z_parts + zh}

    def block_at(dy):
        return pl.multiple_of(((y + dy) % Y_PARTS) * rows, rows)

    partner = {"group": y * z_parts + (1 - zh)}
    up, down = peer(1), peer(Y_PARTS - 1)
    barrier = pltpu.get_barrier_semaphore()
    for dev in (up, down, partner):
        pl.semaphore_signal(barrier, inc=1, device_id=dev, device_id_type=mesh_id)
    pl.semaphore_wait(barrier, 3)

    def remote(src, dst, k, dev):
        c = pltpu.make_async_remote_copy(
            src_ref=src, dst_ref=dst, send_sem=send_sem.at[k], recv_sem=recv_sem.at[k],
            device_id=dev, device_id_type=mesh_id,
        )
        c.start()
        return c

    far = block_at(2)
    first = [
        remote(x_ref.at[pl.ds(block_at(1), rows)], ybuf.at[0], 0, up),
        remote(x_ref.at[pl.ds(block_at(-1), rows)], ybuf.at[1], 1, down),
        remote(x_ref.at[pl.ds(far, half)], fwd.at[0], 2, up),
        remote(x_ref.at[pl.ds(far + half, half)], fwd.at[1], 3, down),
    ]
    local = pltpu.make_async_copy(x_ref.at[pl.ds(block_at(0), rows)], own, local_sem.at[0])
    local.start()
    for c in first:
        c.wait()
    second = [
        remote(fwd.at[0], relay.at[pl.ds(0, half)], 4, up),
        remote(fwd.at[1], relay.at[pl.ds(half, half)], 5, down),
    ]
    local.wait()

    f32 = jnp.float32

    def near_sum(lo):
        sl = pl.ds(lo, half)
        return own[sl, :].astype(f32) + ybuf[0, sl, :].astype(f32) + ybuf[1, sl, :].astype(f32)

    other_lo = pl.multiple_of((1 - zh) * half, half)
    mine_lo = pl.multiple_of(zh * half, half)
    out_ref[...] = near_sum(other_lo)
    for c in second:
        c.wait()
    zsend[...] = (out_ref[...] + relay[pl.ds(other_lo, half), :].astype(f32)).astype(zsend.dtype)
    zc = remote(zsend, zrecv, 6, partner)
    out_ref[...] = near_sum(mine_lo) + relay[pl.ds(mine_lo, half), :].astype(f32)
    zc.wait()
    out_ref[...] += zrecv[...].astype(f32)


def group_reduce_scatter(x, collective_id=0):
    size = lax.axis_size("group")
    r, c = x.shape
    rows = r // Y_PARTS
    half = rows // 2
    return pl.pallas_call(
        _rs_kernel,
        out_shape=jax.ShapeDtypeStruct((r // size, c), jnp.float32),
        in_specs=[pl.BlockSpec(memory_space=pl.ANY)],
        out_specs=pl.BlockSpec(memory_space=pltpu.VMEM),
        scratch_shapes=[
            pltpu.VMEM((2, rows, c), x.dtype),
            pltpu.VMEM((2, half, c), x.dtype),
            pltpu.VMEM((rows, c), x.dtype),
            pltpu.VMEM((rows, c), x.dtype),
            pltpu.VMEM((half, c), x.dtype),
            pltpu.VMEM((half, c), x.dtype),
            pltpu.SemaphoreType.DMA((7,)),
            pltpu.SemaphoreType.DMA((7,)),
            pltpu.SemaphoreType.DMA((1,)),
        ],
        compiler_params=pltpu.CompilerParams(
            collective_id=collective_id, has_side_effects=True, vmem_limit_bytes=48 * 1024 * 1024
        ),
    )(x)


def _ag_kernel(h_ref, out_ref, pbuf, ybuf, fbuf, send_sem, recv_sem):
    size = lax.axis_size("group")
    z_parts = size // Y_PARTS
    j = lax.axis_index("group")
    y, zh = j // z_parts, j % z_parts
    n = h_ref.shape[0]
    mesh_id = pl.DeviceIdType.MESH

    def peer(dy):
        return {"group": ((y + dy) % Y_PARTS) * z_parts + zh}

    partner = {"group": y * z_parts + (1 - zh)}
    up, down = peer(1), peer(Y_PARTS - 1)
    barrier = pltpu.get_barrier_semaphore()
    for dev in (up, down, partner):
        pl.semaphore_signal(barrier, inc=1, device_id=dev, device_id_type=mesh_id)
    pl.semaphore_wait(barrier, 3)

    def remote(src, dst, k, dev):
        c = pltpu.make_async_remote_copy(
            src_ref=src, dst_ref=dst, send_sem=send_sem.at[k], recv_sem=recv_sem.at[k],
            device_id=dev, device_id_type=mesh_id,
        )
        c.start()
        return c

    own_lo = pl.multiple_of(zh * n, n)
    other_lo = pl.multiple_of((1 - zh) * n, n)
    zc = remote(h_ref, pbuf, 0, partner)
    first = [
        remote(h_ref, ybuf.at[0, pl.ds(own_lo, n)], 1, up),
        remote(h_ref, ybuf.at[1, pl.ds(own_lo, n)], 2, down),
    ]
    zc.wait()
    first += [
        remote(pbuf, ybuf.at[0, pl.ds(other_lo, n)], 3, up),
        remote(pbuf, ybuf.at[1, pl.ds(other_lo, n)], 4, down),
    ]
    for c in first:
        c.wait()
    second = [
        remote(ybuf.at[0, pl.ds(0, n)], fbuf.at[0], 5, up),
        remote(ybuf.at[1, pl.ds(n, n)], fbuf.at[1], 6, down),
    ]
    pair = 2 * n

    def at(dy):
        return pl.multiple_of(((y + dy) % Y_PARTS) * pair, pair)

    out_ref[pl.ds(at(0) + own_lo, n), :] = h_ref[...]
    out_ref[pl.ds(at(0) + other_lo, n), :] = pbuf[...]
    out_ref[pl.ds(at(-1), pair), :] = ybuf[0]
    out_ref[pl.ds(at(1), pair), :] = ybuf[1]
    for c in second:
        c.wait()
    out_ref[pl.ds(at(2), n), :] = fbuf[0]
    out_ref[pl.ds(at(2) + n, n), :] = fbuf[1]


def group_all_gather(h, collective_id=0):
    size = lax.axis_size("group")
    n, c = h.shape
    return pl.pallas_call(
        _ag_kernel,
        out_shape=jax.ShapeDtypeStruct((size * n, c), h.dtype),
        in_specs=[pl.BlockSpec(memory_space=pltpu.VMEM)],
        out_specs=pl.BlockSpec(memory_space=pltpu.VMEM),
        scratch_shapes=[
            pltpu.VMEM((n, c), h.dtype),
            pltpu.VMEM((2, 2 * n, c), h.dtype),
            pltpu.VMEM((2, n, c), h.dtype),
            pltpu.SemaphoreType.DMA((7,)),
            pltpu.SemaphoreType.DMA((7,)),
        ],
        compiler_params=pltpu.CompilerParams(
            collective_id=collective_id, has_side_effects=True, vmem_limit_bytes=32 * 1024 * 1024
        ),
    )(h)


def on_device(tokens, proj_in, proj_out, expert_list, block_pattern, route_weight):
    group_size = lax.axis_size("group")
    n_dp = lax.axis_size("dp")
    dp_index = lax.axis_index("dp")
    row_count, width_here = tokens.shape
    slots = expert_list.shape[1]
    ff_here = proj_in.shape[1]
    block_rows = row_count // block_pattern.shape[2]

    own_pattern = lax.dynamic_index_in_dim(block_pattern, dp_index, 0, keepdims=False)
    block_mask = jnp.repeat(own_pattern, block_rows, axis=1).astype(jnp.float32)
    token_scale = route_weight.T * block_mask

    send_out = jnp.take(proj_out, expert_list, axis=0, mode="clip")

    hiddens = []
    pending = tokens
    for slot in range(slots):
        piece = jnp.take(proj_in, expert_list[:, slot], axis=0, mode="clip").transpose(0, 2, 1, 3)
        pending, piece = lax.optimization_barrier((pending, piece))
        weight_in = lax.all_to_all(piece, "dp", 0, 0, tiled=True).reshape(-1, width_here)
        if hiddens:
            previous = hiddens.pop()
            if slot == slots - 1:
                weight_in, previous, send_out = lax.optimization_barrier((weight_in, previous, send_out))
                weights_out = lax.all_to_all(send_out, "dp", 0, 0, tiled=True)
            gathered = group_all_gather(previous, collective_id=slots + slot - 1)
            weight_in, gathered = lax.optimization_barrier((weight_in, gathered))
            hiddens.append(gathered)
        partial_here = jnp.dot(weight_in, tokens.T, preferred_element_type=jnp.float32)
        partial_here = partial_here.astype(jnp.bfloat16)
        shares = group_reduce_scatter(partial_here, collective_id=slot)
        shares = shares.reshape(n_dp // group_size, 2, ff_here, row_count)
        hidden = (token_scale[slot] * jax.nn.silu(shares[:, 0]) * shares[:, 1]).astype(jnp.bfloat16)
        hiddens.append(hidden.reshape(-1, row_count))
        pending = partial_here
    hiddens[-1] = group_all_gather(hiddens[-1], collective_id=2 * slots - 1)
    weights_out = weights_out.reshape(n_dp, slots, -1, width_here)

    combined = None
    for slot in range(slots):
        term = lax.dot_general(
            hiddens[slot], weights_out[:, slot].reshape(-1, width_here), (((0,), (0,)), ((), ())),
            preferred_element_type=jnp.float32,
        )
        combined = term if combined is None else combined + term
    return combined.astype(jnp.bfloat16)


def solution(mesh):
    return jax.shard_map(
        on_device,
        mesh=mesh,
        in_specs=(
            P("dp", "group"),
            P(None, "dp", None, "group"),
            P(None, "dp", "group"),
            P(),
            P(),
            P("dp", None),
        ),
        out_specs=P("dp", "group"),
        check_vma=False,
    )
```

```python
import jax
import jax.numpy as jnp
from jax import lax
from jax.experimental import pallas as pl
from jax.experimental.pallas import tpu as pltpu
from jax.sharding import PartitionSpec as P


Y_PARTS = 4


def _rs_kernel(x_ref, out_ref, ybuf, fwd, relay, own, zsend, zrecv, send_sem, recv_sem, local_sem):
    size = lax.axis_size("group")
    z_parts = size // Y_PARTS
    j = lax.axis_index("group")
    y, zh = j // z_parts, j % z_parts
    rows = x_ref.shape[0] // Y_PARTS
    half = rows // 2
    mesh_id = pl.DeviceIdType.MESH

    def peer(dy):
        return {"group": ((y + dy) % Y_PARTS) * z_parts + zh}

    def block_at(dy):
        return pl.multiple_of(((y + dy) % Y_PARTS) * rows, rows)

    partner = {"group": y * z_parts + (1 - zh)}
    up, down = peer(1), peer(Y_PARTS - 1)
    barrier = pltpu.get_barrier_semaphore()
    for dev in (up, down, partner):
        pl.semaphore_signal(barrier, inc=1, device_id=dev, device_id_type=mesh_id)
    pl.semaphore_wait(barrier, 3)

    def remote(src, dst, k, dev):
        c = pltpu.make_async_remote_copy(
            src_ref=src, dst_ref=dst, send_sem=send_sem.at[k], recv_sem=recv_sem.at[k],
            device_id=dev, device_id_type=mesh_id,
        )
        c.start()
        return c

    far = block_at(2)
    first = [
        remote(x_ref.at[pl.ds(block_at(1), rows)], ybuf.at[0], 0, up),
        remote(x_ref.at[pl.ds(block_at(-1), rows)], ybuf.at[1], 1, down),
        remote(x_ref.at[pl.ds(far, half)], fwd.at[0], 2, up),
        remote(x_ref.at[pl.ds(far + half, half)], fwd.at[1], 3, down),
    ]
    local = pltpu.make_async_copy(x_ref.at[pl.ds(block_at(0), rows)], own, local_sem.at[0])
    local.start()
    for c in first:
        c.wait()
    second = [
        remote(fwd.at[0], relay.at[pl.ds(0, half)], 4, up),
        remote(fwd.at[1], relay.at[pl.ds(half, half)], 5, down),
    ]
    local.wait()

    f32 = jnp.float32

    def near_sum(lo):
        sl = pl.ds(lo, half)
        return own[sl, :].astype(f32) + ybuf[0, sl, :].astype(f32) + ybuf[1, sl, :].astype(f32)

    other_lo = pl.multiple_of((1 - zh) * half, half)
    mine_lo = pl.multiple_of(zh * half, half)
    out_ref[...] = near_sum(other_lo)
    for c in second:
        c.wait()
    zsend[...] = (out_ref[...] + relay[pl.ds(other_lo, half), :].astype(f32)).astype(zsend.dtype)
    zc = remote(zsend, zrecv, 6, partner)
    out_ref[...] = near_sum(mine_lo) + relay[pl.ds(mine_lo, half), :].astype(f32)
    zc.wait()
    out_ref[...] += zrecv[...].astype(f32)


def group_reduce_scatter(x, collective_id=0):
    size = lax.axis_size("group")
    r, c = x.shape
    rows = r // Y_PARTS
    half = rows // 2
    return pl.pallas_call(
        _rs_kernel,
        out_shape=jax.ShapeDtypeStruct((r // size, c), jnp.float32),
        in_specs=[pl.BlockSpec(memory_space=pl.ANY)],
        out_specs=pl.BlockSpec(memory_space=pltpu.VMEM),
        scratch_shapes=[
            pltpu.VMEM((2, rows, c), x.dtype),
            pltpu.VMEM((2, half, c), x.dtype),
            pltpu.VMEM((rows, c), x.dtype),
            pltpu.VMEM((rows, c), x.dtype),
            pltpu.VMEM((half, c), x.dtype),
            pltpu.VMEM((half, c), x.dtype),
            pltpu.SemaphoreType.DMA((7,)),
            pltpu.SemaphoreType.DMA((7,)),
            pltpu.SemaphoreType.DMA((1,)),
        ],
        compiler_params=pltpu.CompilerParams(
            collective_id=collective_id, has_side_effects=True, vmem_limit_bytes=48 * 1024 * 1024
        ),
    )(x)


def _ag_kernel(h_ref, out_ref, pbuf, ybuf, fbuf, send_sem, recv_sem):
    size = lax.axis_size("group")
    z_parts = size // Y_PARTS
    j = lax.axis_index("group")
    y, zh = j // z_parts, j % z_parts
    n = h_ref.shape[0]
    mesh_id = pl.DeviceIdType.MESH

    def peer(dy):
        return {"group": ((y + dy) % Y_PARTS) * z_parts + zh}

    partner = {"group": y * z_parts + (1 - zh)}
    up, down = peer(1), peer(Y_PARTS - 1)
    barrier = pltpu.get_barrier_semaphore()
    for dev in (up, down, partner):
        pl.semaphore_signal(barrier, inc=1, device_id=dev, device_id_type=mesh_id)
    pl.semaphore_wait(barrier, 3)

    def remote(src, dst, k, dev):
        c = pltpu.make_async_remote_copy(
            src_ref=src, dst_ref=dst, send_sem=send_sem.at[k], recv_sem=recv_sem.at[k],
            device_id=dev, device_id_type=mesh_id,
        )
        c.start()
        return c

    own_lo = pl.multiple_of(zh * n, n)
    other_lo = pl.multiple_of((1 - zh) * n, n)
    zc = remote(h_ref, pbuf, 0, partner)
    first = [
        remote(h_ref, ybuf.at[0, pl.ds(own_lo, n)], 1, up),
        remote(h_ref, ybuf.at[1, pl.ds(own_lo, n)], 2, down),
    ]
    zc.wait()
    first += [
        remote(pbuf, ybuf.at[0, pl.ds(other_lo, n)], 3, up),
        remote(pbuf, ybuf.at[1, pl.ds(other_lo, n)], 4, down),
    ]
    for c in first:
        c.wait()
    second = [
        remote(ybuf.at[0, pl.ds(0, n)], fbuf.at[0], 5, up),
        remote(ybuf.at[1, pl.ds(n, n)], fbuf.at[1], 6, down),
    ]
    pair = 2 * n

    def at(dy):
        return pl.multiple_of(((y + dy) % Y_PARTS) * pair, pair)

    out_ref[pl.ds(at(0) + own_lo, n), :] = h_ref[...]
    out_ref[pl.ds(at(0) + other_lo, n), :] = pbuf[...]
    out_ref[pl.ds(at(-1), pair), :] = ybuf[0]
    out_ref[pl.ds(at(1), pair), :] = ybuf[1]
    for c in second:
        c.wait()
    out_ref[pl.ds(at(2), n), :] = fbuf[0]
    out_ref[pl.ds(at(2) + n, n), :] = fbuf[1]


def group_all_gather(h, collective_id=0):
    size = lax.axis_size("group")
    n, c = h.shape
    return pl.pallas_call(
        _ag_kernel,
        out_shape=jax.ShapeDtypeStruct((size * n, c), h.dtype),
        in_specs=[pl.BlockSpec(memory_space=pltpu.VMEM)],
        out_specs=pl.BlockSpec(memory_space=pltpu.VMEM),
        scratch_shapes=[
            pltpu.VMEM((n, c), h.dtype),
            pltpu.VMEM((2, 2 * n, c), h.dtype),
            pltpu.VMEM((2, n, c), h.dtype),
            pltpu.SemaphoreType.DMA((7,)),
            pltpu.SemaphoreType.DMA((7,)),
        ],
        compiler_params=pltpu.CompilerParams(
            collective_id=collective_id, has_side_effects=True, vmem_limit_bytes=32 * 1024 * 1024
        ),
    )(h)


def on_device(tokens, proj_in, proj_out, expert_list, block_pattern, route_weight):
    group_size = lax.axis_size("group")
    n_dp = lax.axis_size("dp")
    dp_index = lax.axis_index("dp")
    row_count, width_here = tokens.shape
    slots = expert_list.shape[1]
    ff_here = proj_in.shape[1]
    block_rows = row_count // block_pattern.shape[2]

    own_pattern = lax.dynamic_index_in_dim(block_pattern, dp_index, 0, keepdims=False)
    block_mask = jnp.repeat(own_pattern, block_rows, axis=1).astype(jnp.float32)
    token_scale = route_weight.T * block_mask

    send_out = jnp.take(proj_out, expert_list, axis=0, mode="clip")

    hiddens = []
    pieces = [
        jnp.take(proj_in, expert_list[:, slot], axis=0, mode="clip").transpose(0, 2, 1, 3)
        for slot in range(slots)
    ]
    weight_in = lax.all_to_all(pieces[0], "dp", 0, 0, tiled=True)
    for slot in range(slots):
        if hiddens:
            weight_in, hiddens[-1] = lax.optimization_barrier((weight_in, hiddens[-1]))
        partial_here = jnp.dot(weight_in.reshape(-1, width_here), tokens.T, preferred_element_type=jnp.float32)
        partial_here = partial_here.astype(jnp.bfloat16)
        if slot == 0:
            partial_here, rest = lax.optimization_barrier((partial_here, pieces[1:] + [send_out]))
            rest = lax.all_to_all(jnp.concatenate(rest, axis=1), "dp", 0, 0, tiled=True)
            later = [rest[:, 2 * k:2 * k + 2] for k in range(slots - 1)]
            weights_out = rest[:, 2 * (slots - 1):]
        shares = group_reduce_scatter(partial_here, collective_id=slot)
        shares = shares.reshape(n_dp // group_size, 2, ff_here, row_count)
        hidden = (token_scale[slot] * jax.nn.silu(shares[:, 0]) * shares[:, 1]).astype(jnp.bfloat16)
        hiddens.append(group_all_gather(hidden.reshape(-1, row_count), collective_id=slots + slot))
        if slot + 1 < slots:
            weight_in = later[slot]

    combined = None
    for slot in range(slots):
        term = lax.dot_general(
            hiddens[slot], weights_out[:, slot].reshape(-1, width_here), (((0,), (0,)), ((), ())),
            preferred_element_type=jnp.float32,
        )
        combined = term if combined is None else combined + term
    return combined.astype(jnp.bfloat16)


def solution(mesh):
    return jax.shard_map(
        on_device,
        mesh=mesh,
        in_specs=(
            P("dp", "group"),
            P(None, "dp", None, "group"),
            P(None, "dp", "group"),
            P(),
            P(),
            P("dp", None),
        ),
        out_specs=P("dp", "group"),
        check_vma=False,
    )
```

```python
import jax
import jax.numpy as jnp
from jax import lax
from jax.experimental import pallas as pl
from jax.experimental.pallas import tpu as pltpu
from jax.sharding import PartitionSpec as P


Y_PARTS = 4


def _rs_kernel(x_ref, out_ref, ybuf, fwd, relay, own, zsend, zrecv, send_sem, recv_sem, local_sem):
    size = lax.axis_size("group")
    z_parts = size // Y_PARTS
    j = lax.axis_index("group")
    y, zh = j // z_parts, j % z_parts
    rows = x_ref.shape[0] // Y_PARTS
    half = rows // 2
    mesh_id = pl.DeviceIdType.MESH

    def peer(dy):
        return {"group": ((y + dy) % Y_PARTS) * z_parts + zh}

    def block_at(dy):
        return pl.multiple_of(((y + dy) % Y_PARTS) * rows, rows)

    partner = {"group": y * z_parts + (1 - zh)}
    up, down = peer(1), peer(Y_PARTS - 1)
    barrier = pltpu.get_barrier_semaphore()
    for dev in (up, down, partner):
        pl.semaphore_signal(barrier, inc=1, device_id=dev, device_id_type=mesh_id)
    pl.semaphore_wait(barrier, 3)

    def remote(src, dst, k, dev):
        c = pltpu.make_async_remote_copy(
            src_ref=src, dst_ref=dst, send_sem=send_sem.at[k], recv_sem=recv_sem.at[k],
            device_id=dev, device_id_type=mesh_id,
        )
        c.start()
        return c

    far = block_at(2)
    first = [
        remote(x_ref.at[pl.ds(block_at(1), rows)], ybuf.at[0], 0, up),
        remote(x_ref.at[pl.ds(block_at(-1), rows)], ybuf.at[1], 1, down),
        remote(x_ref.at[pl.ds(far, half)], fwd.at[0], 2, up),
        remote(x_ref.at[pl.ds(far + half, half)], fwd.at[1], 3, down),
    ]
    local = pltpu.make_async_copy(x_ref.at[pl.ds(block_at(0), rows)], own, local_sem.at[0])
    local.start()
    for c in first:
        c.wait()
    second = [
        remote(fwd.at[0], relay.at[pl.ds(0, half)], 4, up),
        remote(fwd.at[1], relay.at[pl.ds(half, half)], 5, down),
    ]
    local.wait()

    f32 = jnp.float32

    def near_sum(lo):
        sl = pl.ds(lo, half)
        return own[sl, :].astype(f32) + ybuf[0, sl, :].astype(f32) + ybuf[1, sl, :].astype(f32)

    other_lo = pl.multiple_of((1 - zh) * half, half)
    mine_lo = pl.multiple_of(zh * half, half)
    out_ref[...] = near_sum(other_lo)
    for c in second:
        c.wait()
    zsend[...] = (out_ref[...] + relay[pl.ds(other_lo, half), :].astype(f32)).astype(zsend.dtype)
    zc = remote(zsend, zrecv, 6, partner)
    out_ref[...] = near_sum(mine_lo) + relay[pl.ds(mine_lo, half), :].astype(f32)
    zc.wait()
    out_ref[...] += zrecv[...].astype(f32)


def group_reduce_scatter(x, collective_id=0):
    size = lax.axis_size("group")
    r, c = x.shape
    rows = r // Y_PARTS
    half = rows // 2
    return pl.pallas_call(
        _rs_kernel,
        out_shape=jax.ShapeDtypeStruct((r // size, c), jnp.float32),
        in_specs=[pl.BlockSpec(memory_space=pl.ANY)],
        out_specs=pl.BlockSpec(memory_space=pltpu.VMEM),
        scratch_shapes=[
            pltpu.VMEM((2, rows, c), x.dtype),
            pltpu.VMEM((2, half, c), x.dtype),
            pltpu.VMEM((rows, c), x.dtype),
            pltpu.VMEM((rows, c), x.dtype),
            pltpu.VMEM((half, c), x.dtype),
            pltpu.VMEM((half, c), x.dtype),
            pltpu.SemaphoreType.DMA((7,)),
            pltpu.SemaphoreType.DMA((7,)),
            pltpu.SemaphoreType.DMA((1,)),
        ],
        compiler_params=pltpu.CompilerParams(
            collective_id=collective_id, has_side_effects=True, vmem_limit_bytes=48 * 1024 * 1024
        ),
    )(x)


def _ag_kernel(h_ref, out_ref, pbuf, ybuf, fbuf, send_sem, recv_sem):
    size = lax.axis_size("group")
    z_parts = size // Y_PARTS
    j = lax.axis_index("group")
    y, zh = j // z_parts, j % z_parts
    n = h_ref.shape[0]
    mesh_id = pl.DeviceIdType.MESH

    def peer(dy):
        return {"group": ((y + dy) % Y_PARTS) * z_parts + zh}

    partner = {"group": y * z_parts + (1 - zh)}
    up, down = peer(1), peer(Y_PARTS - 1)
    barrier = pltpu.get_barrier_semaphore()
    for dev in (up, down, partner):
        pl.semaphore_signal(barrier, inc=1, device_id=dev, device_id_type=mesh_id)
    pl.semaphore_wait(barrier, 3)

    def remote(src, dst, k, dev):
        c = pltpu.make_async_remote_copy(
            src_ref=src, dst_ref=dst, send_sem=send_sem.at[k], recv_sem=recv_sem.at[k],
            device_id=dev, device_id_type=mesh_id,
        )
        c.start()
        return c

    own_lo = pl.multiple_of(zh * n, n)
    other_lo = pl.multiple_of((1 - zh) * n, n)
    zc = remote(h_ref, pbuf, 0, partner)
    first = [
        remote(h_ref, ybuf.at[0, pl.ds(own_lo, n)], 1, up),
        remote(h_ref, ybuf.at[1, pl.ds(own_lo, n)], 2, down),
    ]
    zc.wait()
    first += [
        remote(pbuf, ybuf.at[0, pl.ds(other_lo, n)], 3, up),
        remote(pbuf, ybuf.at[1, pl.ds(other_lo, n)], 4, down),
    ]
    for c in first:
        c.wait()
    second = [
        remote(ybuf.at[0, pl.ds(0, n)], fbuf.at[0], 5, up),
        remote(ybuf.at[1, pl.ds(n, n)], fbuf.at[1], 6, down),
    ]
    pair = 2 * n

    def at(dy):
        return pl.multiple_of(((y + dy) % Y_PARTS) * pair, pair)

    out_ref[pl.ds(at(0) + own_lo, n), :] = h_ref[...]
    out_ref[pl.ds(at(0) + other_lo, n), :] = pbuf[...]
    out_ref[pl.ds(at(-1), pair), :] = ybuf[0]
    out_ref[pl.ds(at(1), pair), :] = ybuf[1]
    for c in second:
        c.wait()
    out_ref[pl.ds(at(2), n), :] = fbuf[0]
    out_ref[pl.ds(at(2) + n, n), :] = fbuf[1]


def group_all_gather(h, collective_id=0):
    size = lax.axis_size("group")
    n, c = h.shape
    return pl.pallas_call(
        _ag_kernel,
        out_shape=jax.ShapeDtypeStruct((size * n, c), h.dtype),
        in_specs=[pl.BlockSpec(memory_space=pltpu.VMEM)],
        out_specs=pl.BlockSpec(memory_space=pltpu.VMEM),
        scratch_shapes=[
            pltpu.VMEM((n, c), h.dtype),
            pltpu.VMEM((2, 2 * n, c), h.dtype),
            pltpu.VMEM((2, n, c), h.dtype),
            pltpu.SemaphoreType.DMA((7,)),
            pltpu.SemaphoreType.DMA((7,)),
        ],
        compiler_params=pltpu.CompilerParams(
            collective_id=collective_id, has_side_effects=True, vmem_limit_bytes=32 * 1024 * 1024
        ),
    )(h)


def on_device(tokens, proj_in, proj_out, expert_list, block_pattern, route_weight):
    group_size = lax.axis_size("group")
    n_dp = lax.axis_size("dp")
    dp_index = lax.axis_index("dp")
    row_count, width_here = tokens.shape
    slots = expert_list.shape[1]
    ff_here = proj_in.shape[1]
    block_rows = row_count // block_pattern.shape[2]

    own_pattern = lax.dynamic_index_in_dim(block_pattern, dp_index, 0, keepdims=False)
    block_mask = jnp.repeat(own_pattern, block_rows, axis=1).astype(jnp.float32)
    token_scale = route_weight.T * block_mask

    send_out = jnp.take(proj_out, expert_list, axis=0, mode="clip")

    hiddens = []
    pending = tokens
    for slot in range(slots):
        piece = jnp.take(proj_in, expert_list[:, slot], axis=0, mode="clip").transpose(0, 2, 1, 3)
        pending, piece = lax.optimization_barrier((pending, piece))
        weight_in = lax.all_to_all(piece, "dp", 0, 0, tiled=True).reshape(-1, width_here)
        if hiddens:
            weight_in, hiddens[-1] = lax.optimization_barrier((weight_in, hiddens[-1]))
        partial_here = jnp.dot(weight_in, tokens.T, preferred_element_type=jnp.float32)
        partial_here = partial_here.astype(jnp.bfloat16)
        shares = group_reduce_scatter(partial_here, collective_id=slot)
        shares = shares.reshape(n_dp // group_size, 2, ff_here, row_count)
        hidden = (token_scale[slot] * jax.nn.silu(shares[:, 0]) * shares[:, 1]).astype(jnp.bfloat16)
        hiddens.append(group_all_gather(hidden.reshape(-1, row_count), collective_id=slots + slot))
        pending = partial_here
    pending, send_out = lax.optimization_barrier((pending, send_out))
    weights_out = lax.all_to_all(send_out, "dp", 0, 0, tiled=True)

    hidden_all = jnp.stack(hiddens).reshape(slots, n_dp, ff_here, row_count)
    combined = lax.dot_general(
        hidden_all, weights_out, (((0, 1, 2), (1, 0, 2)), ((), ())),
        preferred_element_type=jnp.float32,
    )
    return combined.astype(jnp.bfloat16)


def solution(mesh):
    return jax.shard_map(
        on_device,
        mesh=mesh,
        in_specs=(
            P("dp", "group"),
            P(None, "dp", None, "group"),
            P(None, "dp", "group"),
            P(),
            P(),
            P("dp", None),
        ),
        out_specs=P("dp", "group"),
        check_vma=False,
    )
```

```python
import jax
import jax.numpy as jnp
from jax import lax
from jax.experimental import pallas as pl
from jax.experimental.pallas import tpu as pltpu
from jax.sharding import PartitionSpec as P


Y_PARTS = 4


def _rs_kernel(x_ref, out_ref, ybuf, fwd, relay, own, zsend, zrecv, send_sem, recv_sem, local_sem):
    size = lax.axis_size("group")
    z_parts = size // Y_PARTS
    j = lax.axis_index("group")
    y, zh = j // z_parts, j % z_parts
    rows = x_ref.shape[0] // Y_PARTS
    half = rows // 2
    mesh_id = pl.DeviceIdType.MESH

    def peer(dy):
        return {"group": ((y + dy) % Y_PARTS) * z_parts + zh}

    def block_at(dy):
        return pl.multiple_of(((y + dy) % Y_PARTS) * rows, rows)

    partner = {"group": y * z_parts + (1 - zh)}
    up, down = peer(1), peer(Y_PARTS - 1)
    barrier = pltpu.get_barrier_semaphore()
    for dev in (up, down, partner):
        pl.semaphore_signal(barrier, inc=1, device_id=dev, device_id_type=mesh_id)
    pl.semaphore_wait(barrier, 3)

    def remote(src, dst, k, dev):
        c = pltpu.make_async_remote_copy(
            src_ref=src, dst_ref=dst, send_sem=send_sem.at[k], recv_sem=recv_sem.at[k],
            device_id=dev, device_id_type=mesh_id,
        )
        c.start()
        return c

    far = block_at(2)
    first = [
        remote(x_ref.at[pl.ds(block_at(1), rows)], ybuf.at[0], 0, up),
        remote(x_ref.at[pl.ds(block_at(-1), rows)], ybuf.at[1], 1, down),
        remote(x_ref.at[pl.ds(far, half)], fwd.at[0], 2, up),
        remote(x_ref.at[pl.ds(far + half, half)], fwd.at[1], 3, down),
    ]
    local = pltpu.make_async_copy(x_ref.at[pl.ds(block_at(0), rows)], own, local_sem.at[0])
    local.start()
    for c in first:
        c.wait()
    second = [
        remote(fwd.at[0], relay.at[pl.ds(0, half)], 4, up),
        remote(fwd.at[1], relay.at[pl.ds(half, half)], 5, down),
    ]
    local.wait()

    f32 = jnp.float32

    def near_sum(lo):
        sl = pl.ds(lo, half)
        return own[sl, :].astype(f32) + ybuf[0, sl, :].astype(f32) + ybuf[1, sl, :].astype(f32)

    other_lo = pl.multiple_of((1 - zh) * half, half)
    mine_lo = pl.multiple_of(zh * half, half)
    out_ref[...] = near_sum(other_lo)
    for c in second:
        c.wait()
    zsend[...] = (out_ref[...] + relay[pl.ds(other_lo, half), :].astype(f32)).astype(zsend.dtype)
    zc = remote(zsend, zrecv, 6, partner)
    out_ref[...] = near_sum(mine_lo) + relay[pl.ds(mine_lo, half), :].astype(f32)
    zc.wait()
    out_ref[...] += zrecv[...].astype(f32)


def group_reduce_scatter(x, collective_id=0):
    size = lax.axis_size("group")
    r, c = x.shape
    rows = r // Y_PARTS
    half = rows // 2
    return pl.pallas_call(
        _rs_kernel,
        out_shape=jax.ShapeDtypeStruct((r // size, c), jnp.float32),
        in_specs=[pl.BlockSpec(memory_space=pl.ANY)],
        out_specs=pl.BlockSpec(memory_space=pltpu.VMEM),
        scratch_shapes=[
            pltpu.VMEM((2, rows, c), x.dtype),
            pltpu.VMEM((2, half, c), x.dtype),
            pltpu.VMEM((rows, c), x.dtype),
            pltpu.VMEM((rows, c), x.dtype),
            pltpu.VMEM((half, c), x.dtype),
            pltpu.VMEM((half, c), x.dtype),
            pltpu.SemaphoreType.DMA((7,)),
            pltpu.SemaphoreType.DMA((7,)),
            pltpu.SemaphoreType.DMA((1,)),
        ],
        compiler_params=pltpu.CompilerParams(
            collective_id=collective_id, has_side_effects=True, vmem_limit_bytes=48 * 1024 * 1024
        ),
    )(x)


def _ag_kernel(h_ref, out_ref, pbuf, ybuf, fbuf, send_sem, recv_sem):
    size = lax.axis_size("group")
    z_parts = size // Y_PARTS
    j = lax.axis_index("group")
    y, zh = j // z_parts, j % z_parts
    n = h_ref.shape[0]
    mesh_id = pl.DeviceIdType.MESH

    def peer(dy):
        return {"group": ((y + dy) % Y_PARTS) * z_parts + zh}

    partner = {"group": y * z_parts + (1 - zh)}
    up, down = peer(1), peer(Y_PARTS - 1)
    barrier = pltpu.get_barrier_semaphore()
    for dev in (up, down, partner):
        pl.semaphore_signal(barrier, inc=1, device_id=dev, device_id_type=mesh_id)
    pl.semaphore_wait(barrier, 3)

    def remote(src, dst, k, dev):
        c = pltpu.make_async_remote_copy(
            src_ref=src, dst_ref=dst, send_sem=send_sem.at[k], recv_sem=recv_sem.at[k],
            device_id=dev, device_id_type=mesh_id,
        )
        c.start()
        return c

    own_lo = pl.multiple_of(zh * n, n)
    other_lo = pl.multiple_of((1 - zh) * n, n)
    zc = remote(h_ref, pbuf, 0, partner)
    first = [
        remote(h_ref, ybuf.at[0, pl.ds(own_lo, n)], 1, up),
        remote(h_ref, ybuf.at[1, pl.ds(own_lo, n)], 2, down),
    ]
    zc.wait()
    first += [
        remote(pbuf, ybuf.at[0, pl.ds(other_lo, n)], 3, up),
        remote(pbuf, ybuf.at[1, pl.ds(other_lo, n)], 4, down),
    ]
    for c in first:
        c.wait()
    second = [
        remote(ybuf.at[0, pl.ds(0, n)], fbuf.at[0], 5, up),
        remote(ybuf.at[1, pl.ds(n, n)], fbuf.at[1], 6, down),
    ]
    pair = 2 * n

    def at(dy):
        return pl.multiple_of(((y + dy) % Y_PARTS) * pair, pair)

    out_ref[pl.ds(at(0) + own_lo, n), :] = h_ref[...]
    out_ref[pl.ds(at(0) + other_lo, n), :] = pbuf[...]
    out_ref[pl.ds(at(-1), pair), :] = ybuf[0]
    out_ref[pl.ds(at(1), pair), :] = ybuf[1]
    for c in second:
        c.wait()
    out_ref[pl.ds(at(2), n), :] = fbuf[0]
    out_ref[pl.ds(at(2) + n, n), :] = fbuf[1]


def group_all_gather(h, collective_id=0):
    size = lax.axis_size("group")
    n, c = h.shape
    return pl.pallas_call(
        _ag_kernel,
        out_shape=jax.ShapeDtypeStruct((size * n, c), h.dtype),
        in_specs=[pl.BlockSpec(memory_space=pltpu.VMEM)],
        out_specs=pl.BlockSpec(memory_space=pltpu.VMEM),
        scratch_shapes=[
            pltpu.VMEM((n, c), h.dtype),
            pltpu.VMEM((2, 2 * n, c), h.dtype),
            pltpu.VMEM((2, n, c), h.dtype),
            pltpu.SemaphoreType.DMA((7,)),
            pltpu.SemaphoreType.DMA((7,)),
        ],
        compiler_params=pltpu.CompilerParams(
            collective_id=collective_id, has_side_effects=True, vmem_limit_bytes=32 * 1024 * 1024
        ),
    )(h)


def on_device(tokens, proj_in, proj_out, expert_list, block_pattern, route_weight):
    group_size = lax.axis_size("group")
    n_dp = lax.axis_size("dp")
    dp_index = lax.axis_index("dp")
    row_count, width_here = tokens.shape
    slots = expert_list.shape[1]
    ff_here = proj_in.shape[1]
    block_rows = row_count // block_pattern.shape[2]

    own_pattern = lax.dynamic_index_in_dim(block_pattern, dp_index, 0, keepdims=False)
    block_mask = jnp.repeat(own_pattern, block_rows, axis=1).astype(jnp.float32)
    token_scale = route_weight.T * block_mask

    send_out = jnp.take(proj_out, expert_list, axis=0, mode="clip")

    hiddens = []
    pending = tokens
    for slot in range(slots):
        piece = jnp.take(proj_in, expert_list[:, slot], axis=0, mode="clip").transpose(0, 2, 1, 3)
        pending, piece = lax.optimization_barrier((pending, piece))
        weight_in = lax.all_to_all(piece, "dp", 0, 0, tiled=True).reshape(-1, width_here)
        if not hiddens:
            weight_in, send_out = lax.optimization_barrier((weight_in, send_out))
        if hiddens:
            weight_in, hiddens[-1] = lax.optimization_barrier((weight_in, hiddens[-1]))
        partial_here = jnp.dot(weight_in, tokens.T, preferred_element_type=jnp.float32)
        partial_here = partial_here.astype(jnp.bfloat16)
        shares = group_reduce_scatter(partial_here, collective_id=slot)
        shares = shares.reshape(n_dp // group_size, 2, ff_here, row_count)
        hidden = (token_scale[slot] * jax.nn.silu(shares[:, 0]) * shares[:, 1]).astype(jnp.bfloat16)
        hiddens.append(group_all_gather(hidden.reshape(-1, row_count), collective_id=slots + slot))
        pending = partial_here
    pending, send_out = lax.optimization_barrier((pending, send_out))
    weights_out = lax.all_to_all(send_out, "dp", 0, 0, tiled=True)

    combined = None
    for slot in range(slots):
        term = lax.dot_general(
            hiddens[slot], weights_out[:, slot].reshape(-1, width_here), (((0,), (0,)), ((), ())),
            preferred_element_type=jnp.float32,
        )
        combined = term if combined is None else combined + term
    return combined.astype(jnp.bfloat16)


def solution(mesh):
    return jax.shard_map(
        on_device,
        mesh=mesh,
        in_specs=(
            P("dp", "group"),
            P(None, "dp", None, "group"),
            P(None, "dp", "group"),
            P(),
            P(),
            P("dp", None),
        ),
        out_specs=P("dp", "group"),
        check_vma=False,
    )
```

```python
import jax
import jax.numpy as jnp
from jax import lax
from jax.experimental import pallas as pl
from jax.experimental.pallas import tpu as pltpu
from jax.sharding import PartitionSpec as P


Y_PARTS = 4


def _rs_kernel(x_ref, out_ref, ybuf, fwd, relay, own, zsend, zrecv, send_sem, recv_sem, local_sem):
    size = lax.axis_size("group")
    z_parts = size // Y_PARTS
    j = lax.axis_index("group")
    y, zh = j // z_parts, j % z_parts
    rows = x_ref.shape[0] // Y_PARTS
    half = rows // 2
    mesh_id = pl.DeviceIdType.MESH

    def peer(dy):
        return {"group": ((y + dy) % Y_PARTS) * z_parts + zh}

    def block_at(dy):
        return pl.multiple_of(((y + dy) % Y_PARTS) * rows, rows)

    partner = {"group": y * z_parts + (1 - zh)}
    up, down = peer(1), peer(Y_PARTS - 1)
    barrier = pltpu.get_barrier_semaphore()
    for dev in (up, down, partner):
        pl.semaphore_signal(barrier, inc=1, device_id=dev, device_id_type=mesh_id)
    pl.semaphore_wait(barrier, 3)

    def remote(src, dst, k, dev):
        c = pltpu.make_async_remote_copy(
            src_ref=src, dst_ref=dst, send_sem=send_sem.at[k], recv_sem=recv_sem.at[k],
            device_id=dev, device_id_type=mesh_id,
        )
        c.start()
        return c

    far = block_at(2)
    first = [
        remote(x_ref.at[pl.ds(block_at(1), rows)], ybuf.at[0], 0, up),
        remote(x_ref.at[pl.ds(block_at(-1), rows)], ybuf.at[1], 1, down),
        remote(x_ref.at[pl.ds(far, half)], fwd.at[0], 2, up),
        remote(x_ref.at[pl.ds(far + half, half)], fwd.at[1], 3, down),
    ]
    local = pltpu.make_async_copy(x_ref.at[pl.ds(block_at(0), rows)], own, local_sem.at[0])
    local.start()
    for c in first:
        c.wait()
    second = [
        remote(fwd.at[0], relay.at[pl.ds(0, half)], 4, up),
        remote(fwd.at[1], relay.at[pl.ds(half, half)], 5, down),
    ]
    local.wait()

    f32 = jnp.float32

    def near_sum(lo):
        sl = pl.ds(lo, half)
        return own[sl, :].astype(f32) + ybuf[0, sl, :].astype(f32) + ybuf[1, sl, :].astype(f32)

    other_lo = pl.multiple_of((1 - zh) * half, half)
    mine_lo = pl.multiple_of(zh * half, half)
    out_ref[...] = near_sum(other_lo)
    for c in second:
        c.wait()
    zsend[...] = (out_ref[...] + relay[pl.ds(other_lo, half), :].astype(f32)).astype(zsend.dtype)
    zc = remote(zsend, zrecv, 6, partner)
    out_ref[...] = near_sum(mine_lo) + relay[pl.ds(mine_lo, half), :].astype(f32)
    zc.wait()
    out_ref[...] += zrecv[...].astype(f32)


def group_reduce_scatter(x, collective_id=0):
    size = lax.axis_size("group")
    r, c = x.shape
    rows = r // Y_PARTS
    half = rows // 2
    return pl.pallas_call(
        _rs_kernel,
        out_shape=jax.ShapeDtypeStruct((r // size, c), jnp.float32),
        in_specs=[pl.BlockSpec(memory_space=pl.ANY)],
        out_specs=pl.BlockSpec(memory_space=pltpu.VMEM),
        scratch_shapes=[
            pltpu.VMEM((2, rows, c), x.dtype),
            pltpu.VMEM((2, half, c), x.dtype),
            pltpu.VMEM((rows, c), x.dtype),
            pltpu.VMEM((rows, c), x.dtype),
            pltpu.VMEM((half, c), x.dtype),
            pltpu.VMEM((half, c), x.dtype),
            pltpu.SemaphoreType.DMA((7,)),
            pltpu.SemaphoreType.DMA((7,)),
            pltpu.SemaphoreType.DMA((1,)),
        ],
        compiler_params=pltpu.CompilerParams(
            collective_id=collective_id, has_side_effects=True, vmem_limit_bytes=48 * 1024 * 1024
        ),
    )(x)


def _ag_kernel(h_ref, out_ref, pbuf, ybuf, fbuf, send_sem, recv_sem):
    size = lax.axis_size("group")
    z_parts = size // Y_PARTS
    j = lax.axis_index("group")
    y, zh = j // z_parts, j % z_parts
    n = h_ref.shape[0]
    mesh_id = pl.DeviceIdType.MESH

    def peer(dy):
        return {"group": ((y + dy) % Y_PARTS) * z_parts + zh}

    partner = {"group": y * z_parts + (1 - zh)}
    up, down = peer(1), peer(Y_PARTS - 1)
    barrier = pltpu.get_barrier_semaphore()
    for dev in (up, down, partner):
        pl.semaphore_signal(barrier, inc=1, device_id=dev, device_id_type=mesh_id)
    pl.semaphore_wait(barrier, 3)

    def remote(src, dst, k, dev):
        c = pltpu.make_async_remote_copy(
            src_ref=src, dst_ref=dst, send_sem=send_sem.at[k], recv_sem=recv_sem.at[k],
            device_id=dev, device_id_type=mesh_id,
        )
        c.start()
        return c

    own_lo = pl.multiple_of(zh * n, n)
    other_lo = pl.multiple_of((1 - zh) * n, n)
    zc = remote(h_ref, pbuf, 0, partner)
    own_up = remote(h_ref, ybuf.at[0, pl.ds(own_lo, n)], 1, up)
    own_down = remote(h_ref, ybuf.at[1, pl.ds(own_lo, n)], 2, down)
    own_up.wait()
    relay_up = remote(ybuf.at[0, pl.ds(own_lo, n)], fbuf.at[0], 5, up)
    zc.wait()
    rest = [
        own_down,
        remote(pbuf, ybuf.at[0, pl.ds(other_lo, n)], 3, up),
        remote(pbuf, ybuf.at[1, pl.ds(other_lo, n)], 4, down),
    ]
    for c in rest:
        c.wait()
    relay_down = remote(ybuf.at[1, pl.ds(other_lo, n)], fbuf.at[1], 6, down)
    pair = 2 * n

    def at(dy):
        return pl.multiple_of(((y + dy) % Y_PARTS) * pair, pair)

    out_ref[pl.ds(at(0) + own_lo, n), :] = h_ref[...]
    out_ref[pl.ds(at(0) + other_lo, n), :] = pbuf[...]
    out_ref[pl.ds(at(-1), pair), :] = ybuf[0]
    out_ref[pl.ds(at(1), pair), :] = ybuf[1]
    relay_up.wait()
    relay_down.wait()
    out_ref[pl.ds(at(2) + own_lo, n), :] = fbuf[0]
    out_ref[pl.ds(at(2) + other_lo, n), :] = fbuf[1]


def group_all_gather(h, collective_id=0):
    size = lax.axis_size("group")
    n, c = h.shape
    return pl.pallas_call(
        _ag_kernel,
        out_shape=jax.ShapeDtypeStruct((size * n, c), h.dtype),
        in_specs=[pl.BlockSpec(memory_space=pltpu.VMEM)],
        out_specs=pl.BlockSpec(memory_space=pltpu.VMEM),
        scratch_shapes=[
            pltpu.VMEM((n, c), h.dtype),
            pltpu.VMEM((2, 2 * n, c), h.dtype),
            pltpu.VMEM((2, n, c), h.dtype),
            pltpu.SemaphoreType.DMA((7,)),
            pltpu.SemaphoreType.DMA((7,)),
        ],
        compiler_params=pltpu.CompilerParams(
            collective_id=collective_id, has_side_effects=True, vmem_limit_bytes=32 * 1024 * 1024
        ),
    )(h)


def on_device(tokens, proj_in, proj_out, expert_list, block_pattern, route_weight):
    group_size = lax.axis_size("group")
    n_dp = lax.axis_size("dp")
    dp_index = lax.axis_index("dp")
    row_count, width_here = tokens.shape
    slots = expert_list.shape[1]
    ff_here = proj_in.shape[1]
    block_rows = row_count // block_pattern.shape[2]

    own_pattern = lax.dynamic_index_in_dim(block_pattern, dp_index, 0, keepdims=False)
    block_mask = jnp.repeat(own_pattern, block_rows, axis=1).astype(jnp.float32)
    token_scale = route_weight.T * block_mask

    send_out = jnp.take(proj_out, expert_list, axis=0, mode="clip")

    hiddens = []
    pending = tokens
    for slot in range(slots):
        piece = jnp.take(proj_in, expert_list[:, slot], axis=0, mode="clip").transpose(0, 2, 1, 3)
        pending, piece = lax.optimization_barrier((pending, piece))
        weight_in = lax.all_to_all(piece, "dp", 0, 0, tiled=True).reshape(-1, width_here)
        if not hiddens:
            weight_in, send_out = lax.optimization_barrier((weight_in, send_out))
        if hiddens:
            weight_in, hiddens[-1] = lax.optimization_barrier((weight_in, hiddens[-1]))
        partial_here = jnp.dot(weight_in, tokens.T, preferred_element_type=jnp.float32)
        partial_here = partial_here.astype(jnp.bfloat16)
        shares = group_reduce_scatter(partial_here, collective_id=slot)
        shares = shares.reshape(n_dp // group_size, 2, ff_here, row_count)
        hidden = (token_scale[slot] * jax.nn.silu(shares[:, 0]) * shares[:, 1]).astype(jnp.bfloat16)
        hiddens.append(group_all_gather(hidden.reshape(-1, row_count), collective_id=slots + slot))
        pending = partial_here
    pending, send_out = lax.optimization_barrier((pending, send_out))
    weights_out = lax.all_to_all(send_out, "dp", 0, 0, tiled=True)

    combined = None
    for slot in range(slots):
        term = lax.dot_general(
            hiddens[slot], weights_out[:, slot].reshape(-1, width_here), (((0,), (0,)), ((), ())),
            preferred_element_type=jnp.float32,
        )
        combined = term if combined is None else combined + term
    return combined.astype(jnp.bfloat16)


def solution(mesh):
    return jax.shard_map(
        on_device,
        mesh=mesh,
        in_specs=(
            P("dp", "group"),
            P(None, "dp", None, "group"),
            P(None, "dp", "group"),
            P(),
            P(),
            P("dp", None),
        ),
        out_specs=P("dp", "group"),
        check_vma=False,
    )
```
